128 devices in a mesh: gz: 32 (over z_lo, y, x), ch: 4 (over z_hi, core).
Axes of the slice: x: 4, y: 4, z: 4 (z_hi: 2, z_lo: 2; z = z_hi * 2 + z_lo), core: 2. Of those that a mesh axis runs over, the one named last changes fastest.
Arguments:
- volume: bfloat16 [128, 64, 16, 128], P('ch', 'gz'), may hold values from -6 to 6
- weight: bfloat16 [27, 128, 128], replicated, may hold values from -0.109375 to 0.109375
- cotangent: bfloat16 [128, 64, 16, 128], P('ch', 'gz'), may hold values from -6 to 6
Outputs:
- output: bfloat16 [128, 64, 16, 128], P('ch', 'gz')
- input_grad: bfloat16 [128, 64, 16, 128], P('ch', 'gz')
- weight_grad: float32 [27, 128, 128], P(None, 'gz', 'ch')
The draws below stay inside these ranges and needn't reach their ends.
All inputs are finite; a program needn't handle non-finite values.
Results may differ from the reference program's by a relative error of at most 0.023.
Values may be sent and summed in bfloat16 or wider, within the bound.
A program may use at most 128 MiB of HBM per device.

```python
import math
import jax
import jax.numpy as jnp
from jax import lax

CIN = 128
COUT = 128
Y = 16
X = 128
Z = 64
VOXELS = 131072


def strengthened(values, own_key, source, target, blocks, factor):
    def block_of(dim):
        return (jnp.arange(values.shape[dim]) // (values.shape[dim] // blocks)).reshape((-1,) + (1,) * (values.ndim - 1 - dim))

    near = jax.random.permutation(own_key, blocks)[block_of(target)]
    second = (block_of(target) + blocks // 2) % blocks
    return jnp.where((block_of(source) == near) | (block_of(source) == second), factor * values, values)


def steps_of(rng, shape, shards, low, top_value):
    loudness = 1.0
    for position, shards_of in shards:
        draws = jax.random.uniform(jax.random.fold_in(jax.random.fold_in(rng, 6), position), (shards_of,), jnp.float32, low / len(shards), top_value / len(shards))
        loudness = loudness * jnp.repeat(jnp.exp(draws), shape[position] // shards_of).reshape((-1,) + (1,) * (len(shape) - 1 - position))
    return loudness


def gaussian(own_key, extent, spread, limit, split=(), held_as=jnp.bfloat16):
    values = jax.random.normal(own_key, extent, jnp.float32) * spread
    if len(split) > 0:
        values = steps_of(own_key, extent, split, -0.22, 0.18) * values
    return jnp.clip(values, min=-limit, max=limit).astype(held_as)


def bell_draw_with(rng, extent, deviation, most, pieces, heavy, kind=jnp.bfloat16):
    values = deviation * jax.random.normal(rng, extent, jnp.float32)
    if pieces:
        values = values * steps_of(rng, extent, pieces, -0.22, 0.18)
    return jnp.clip(strengthened(values, jax.random.fold_in(rng, 3), *heavy), -most, most).astype(kind)


def setup_inputs(seed: int = 0) -> dict:
    key_list = jax.random.split(jax.random.key(seed), 4)
    volume = bell_draw_with(key_list[0], (CIN, Z, Y, X), 1.0, 6.0, ((0, 4), (1, 32)), (1, 0, 32, 2.75))
    weight = gaussian(key_list[1], (27, CIN, COUT), (27 * CIN) ** -0.5, 0.109375)
    cotangent = gaussian(key_list[2], (COUT, Z, Y, X), 1.0, 6.0, ((0, 4), (1, 32)))
    return dict(volume=volume, weight=weight, cotangent=cotangent)


def convolve(field, kernel):
    return lax.conv_general_dilated(field, kernel, (1, 1, 1), 'SAME', dimension_numbers=('NCDHW', 'DHWIO', 'NCDHW'), precision=lax.Precision.HIGHEST)

def reference(volume, weight, cotangent):
    field = volume.astype(jnp.float32)[None]
    kernel = weight.astype(jnp.float32).reshape(3, 3, 3, CIN, COUT)
    result, pullback = jax.vjp(convolve, field, kernel)
    field_grad, kernel_grad = pullback(cotangent.astype(jnp.float32)[None])
    output = result[0].astype(jnp.bfloat16)
    input_grad = field_grad[0].astype(jnp.bfloat16)
    weight_grad = kernel_grad.reshape(27, CIN, COUT) * jnp.float32(1.0 / math.sqrt(VOXELS))
    return (output, input_grad, weight_grad)
```

```python
import math

import jax
import jax.numpy as jnp
from jax import lax
from jax.sharding import PartitionSpec as P


def with_halo(shard, axis, dim):
    devices, length = lax.axis_size(axis), shard.shape[dim]
    up = [(i, i + 1) for i in range(devices - 1)]
    down = [(j, i) for i, j in up]
    last = lax.slice_in_dim(shard, length - 1, length, axis=dim)
    first = lax.slice_in_dim(shard, 0, 1, axis=dim)
    before = lax.ppermute(last, axis, up)
    after = lax.ppermute(first, axis, down)
    return jnp.concatenate([before, shard, after], axis=dim)


SAME_YX = ((0, 0), (1, 1), (1, 1))


def body(volume, weight, cotangent):
    in_local, planes_local, grid_rows, grid_cols = volume.shape
    out_local = cotangent.shape[0]
    groups = lax.axis_size("ch")
    my_group = lax.axis_index("ch")
    voxels = planes_local * lax.axis_size("gz") * grid_rows * grid_cols

    both = jnp.concatenate([volume, cotangent], axis=0)
    padded = with_halo(both, "gz", 1)
    gathered = lax.all_gather(padded, "ch", axis=0)
    planes = padded.shape[1]
    vol_full = gathered[:, :in_local].reshape(groups * in_local, planes, grid_rows, grid_cols)
    cot_full = gathered[:, in_local:].reshape(groups * out_local, planes, grid_rows, grid_cols)
    cin = vol_full.shape[0]
    cout = cot_full.shape[0]

    weight_cols = lax.dynamic_slice_in_dim(weight, my_group * out_local, out_local, 2)
    out = lax.conv_general_dilated(
        vol_full[None],
        weight_cols.reshape(3, 3, 3, cin, out_local),
        (1, 1, 1),
        SAME_YX,
        dimension_numbers=("NCDHW", "DHWIO", "NCDHW"),
        preferred_element_type=jnp.float32,
    )[0]

    weight_rows = lax.dynamic_slice_in_dim(weight, my_group * in_local, in_local, 1)
    flipped = jnp.swapaxes(weight_rows[::-1], 1, 2).reshape(3, 3, 3, cout, in_local)
    cot_padded = cot_full[None]
    in_grad = lax.conv_general_dilated(
        cot_padded,
        flipped,
        (1, 1, 1),
        SAME_YX,
        dimension_numbers=("NCDHW", "DHWIO", "NCDHW"),
        preferred_element_type=jnp.float32,
    )[0]

    wpart = lax.conv_general_dilated(
        vol_full[None],
        cotangent[None],
        (1, 1, 1),
        SAME_YX,
        dimension_numbers=("CNDHW", "IODHW", "NCDHW"),
        preferred_element_type=jnp.float32,
    )
    wpart = jnp.transpose(wpart, (2, 3, 4, 0, 1)).reshape(27, cin, out_local)
    wgrad = lax.psum_scatter(wpart, "gz", scatter_dimension=1, tiled=True)
    wgrad = wgrad * jnp.float32(1.0 / math.sqrt(voxels))
    return out.astype(jnp.bfloat16), in_grad.astype(jnp.bfloat16), wgrad


def solution(mesh):
    placed = P("ch", "gz", None, None)
    return jax.shard_map(
        body,
        mesh=mesh,
        in_specs=(placed, P(), placed),
        out_specs=(placed, placed, P(None, "gz", "ch")),
        check_vma=False,
    )
```

```python
import math

import jax
import jax.numpy as jnp
from jax import lax
from jax.sharding import PartitionSpec as P


def with_halo(shard, axis, dim):
    devices, length = lax.axis_size(axis), shard.shape[dim]
    up = [(i, i + 1) for i in range(devices - 1)]
    down = [(j, i) for i, j in up]
    last = lax.slice_in_dim(shard, length - 1, length, axis=dim)
    first = lax.slice_in_dim(shard, 0, 1, axis=dim)
    before = lax.ppermute(last, axis, up)
    after = lax.ppermute(first, axis, down)
    return jnp.concatenate([before, shard, after], axis=dim)


def shift_x(field, step):
    pads = [(0, 0, 0)] * (field.ndim - 1) + [(-step, step, 0)]
    return lax.pad(field, jnp.zeros((), field.dtype), pads)


def from_everyone(shard, axis):
    copies = jnp.broadcast_to(shard, (lax.axis_size(axis), *shard.shape))
    return lax.all_to_all(copies, axis, split_axis=0, concat_axis=0, tiled=True)


def conv_taps(padded, matrices, planes_local, grid_rows, flipped):
    summed = None
    for tap_z in range(3):
        for tap_y in range(3):
            for tap_x in range(3):
                low_z = 2 - tap_z if flipped else tap_z
                low_y = 2 - tap_y if flipped else tap_y
                step = 1 - tap_x if flipped else tap_x - 1
                segment = shift_x(
                    padded[:, low_z : low_z + planes_local, low_y : low_y + grid_rows, :], step
                )
                contrib = jnp.einsum(
                    "czyx,cd->dzyx",
                    segment,
                    matrices[9 * tap_z + 3 * tap_y + tap_x],
                    preferred_element_type=jnp.float32,
                )
                summed = contrib if summed is None else summed + contrib
    return summed


def weight_taps(vol_full, cotangent, planes_local):
    shifted = []
    for tap_y in range(3):
        for tap_x in range(3):
            rows = jnp.pad(cotangent, ((0, 0), (0, 0), (tap_y, 2 - tap_y), (0, 0)))
            shifted.append(shift_x(rows, 1 - tap_x))
    stack = jnp.stack(shifted, axis=0)
    parts = []
    for tap_z in range(3):
        slab = vol_full[:, tap_z : tap_z + planes_local]
        parts.append(
            jnp.einsum("izyx,tozyx->ito", slab, stack, preferred_element_type=jnp.float32)
        )
    return jnp.concatenate(parts, axis=1)


def body(volume, weight, cotangent):
    in_local, planes_local, grid_rows, grid_cols = volume.shape
    out_local = cotangent.shape[0]
    groups = lax.axis_size("ch")
    slabs = lax.axis_size("gz")
    my_group = lax.axis_index("ch")
    voxels = planes_local * slabs * grid_rows * grid_cols

    both = jnp.concatenate([volume, cotangent], axis=0)
    padded = with_halo(both, "gz", 1)
    padded = jnp.pad(padded, ((0, 0), (0, 0), (1, 1), (0, 0)))
    gathered = from_everyone(padded, "ch")
    vol_full = gathered[:, :in_local].reshape(groups * in_local, *padded.shape[1:])
    cot_full = gathered[:, in_local:].reshape(groups * out_local, *padded.shape[1:])
    cin = vol_full.shape[0]

    wpart = weight_taps(vol_full, cotangent, planes_local).astype(jnp.bfloat16)
    blocks = wpart.reshape(slabs, cin // slabs, *wpart.shape[1:])
    arrived = lax.all_to_all(blocks, "gz", split_axis=0, concat_axis=0, tiled=True)
    wgrad = arrived.astype(jnp.float32).sum(axis=0)
    wgrad = jnp.transpose(wgrad, (1, 0, 2)) * jnp.float32(1.0 / math.sqrt(voxels))

    weight_cols = lax.dynamic_slice_in_dim(weight, my_group * out_local, out_local, 2)
    out = conv_taps(vol_full, weight_cols, planes_local, grid_rows, False)
    weight_rows = lax.dynamic_slice_in_dim(weight, my_group * in_local, in_local, 1)
    in_grad = conv_taps(
        cot_full, jnp.swapaxes(weight_rows, 1, 2), planes_local, grid_rows, True
    )
    return out.astype(jnp.bfloat16), in_grad.astype(jnp.bfloat16), wgrad


def solution(mesh):
    placed = P("ch", "gz", None, None)
    return jax.shard_map(
        body,
        mesh=mesh,
        in_specs=(placed, P(), placed),
        out_specs=(placed, placed, P(None, "gz", "ch")),
        check_vma=False,
    )
```

```python
import math

import jax
import jax.numpy as jnp
from jax import lax
from jax.sharding import Mesh
from jax.sharding import PartitionSpec as P

CH = ("ch_0", "ch_1")


def padded_2(shard, sides, width):
    for axis, dim in sides:
        devices, length = (lax.axis_size(axis), shard.shape[dim])
        up = [(i, (i + 1) % devices) for i in range(devices - 1)]
        down = [(j, i) for i, j in up]
        last = lax.slice_in_dim(shard, length - width, length, axis=dim)
        first = lax.slice_in_dim(shard, 0, width, axis=dim)
        before = lax.ppermute(last, axis, up)
        after = lax.ppermute(first, axis, down)
        shard = jnp.concatenate([before, shard, after], axis=dim)
    return shard


def from_everyone(shard, axis):
    copies = jnp.broadcast_to(shard, (lax.axis_size(axis), *shard.shape))
    return lax.all_to_all(copies, axis, split_axis=0, concat_axis=0, tiled=True)


def in_order(blocks, dim):
    lengths = list(blocks.shape[1:])
    lengths[dim] *= blocks.shape[0]
    return jnp.moveaxis(blocks, 0, dim).reshape(lengths)


def gathered_by_axis(shard, axes, dim):
    far, near = axes
    blocks = from_everyone(from_everyone(shard, far), near)
    return in_order(blocks.swapaxes(0, 1).reshape(-1, *shard.shape), dim)


def in_blocks(shard, dim, devices):
    before, after = (shard.shape[:dim], shard.shape[dim + 1 :])
    return jnp.moveaxis(shard.reshape(*before, devices, -1, *after), dim, 0)


def summed_on_arrival(shard, axis, dim):
    blocks = in_blocks(shard, dim, lax.axis_size(axis))
    arrived = lax.all_to_all(blocks, axis, split_axis=0, concat_axis=0, tiled=True)
    return arrived.astype(jnp.float32).sum(axis=0)


def widen(field):
    return jnp.pad(field, ((0, 0), (0, 0), (1, 1), (1, 1)))


def conv_taps(padded, matrices, planes_local, flipped):
    grid_rows = padded.shape[2] - 2
    grid_cols = padded.shape[3] - 2
    summed = None
    for tap_z in range(3):
        for tap_y in range(3):
            for tap_x in range(3):
                low_z = 2 - tap_z if flipped else tap_z
                low_y = 2 - tap_y if flipped else tap_y
                low_x = 2 - tap_x if flipped else tap_x
                segment = padded[
                    :,
                    low_z : low_z + planes_local,
                    low_y : low_y + grid_rows,
                    low_x : low_x + grid_cols,
                ]
                contrib = jnp.einsum(
                    "czyx,cd->dzyx",
                    segment,
                    matrices[9 * tap_z + 3 * tap_y + tap_x],
                    preferred_element_type=jnp.float32,
                )
                summed = contrib if summed is None else summed + contrib
    return summed


def tap_products(padded, gradient, planes_local):
    grid_rows = gradient.shape[2]
    grid_cols = gradient.shape[3]
    stacked = []
    for tap_z in range(3):
        for tap_y in range(3):
            for tap_x in range(3):
                segment = padded[
                    :,
                    tap_z : tap_z + planes_local,
                    tap_y : tap_y + grid_rows,
                    tap_x : tap_x + grid_cols,
                ]
                stacked.append(
                    jnp.einsum(
                        "czyx,dzyx->cd", segment, gradient, preferred_element_type=jnp.float32
                    )
                )
    return jnp.stack(stacked, axis=0)


def body(volume, weight, cotangent):
    in_local, planes_local, grid_rows, grid_cols = volume.shape
    out_local = cotangent.shape[0]
    my_group = lax.axis_index(CH)
    voxels = planes_local * lax.axis_size("gz") * grid_rows * grid_cols
    both = padded_2(jnp.concatenate([volume, cotangent], axis=0), (("gz", 1),), 1)
    far, near = CH
    blocks = from_everyone(from_everyone(both, far), near)
    blocks = blocks.swapaxes(0, 1).reshape(-1, *both.shape)
    vol_full = blocks[:, :in_local].reshape(-1, *both.shape[1:])
    cot_full = blocks[:, in_local:].reshape(-1, *both.shape[1:])
    weight_cols = lax.dynamic_slice_in_dim(weight, my_group * out_local, out_local, 2)
    padded = widen(vol_full)
    out_acc = conv_taps(padded, weight_cols, planes_local, False)
    weight_acc = tap_products(padded, cotangent, planes_local)
    weight_grad = summed_on_arrival(weight_acc.astype(jnp.bfloat16), "gz", 1) * jnp.float32(
        1.0 / math.sqrt(voxels)
    )
    weight_rows = lax.dynamic_slice_in_dim(weight, my_group * in_local, in_local, 1)
    input_acc = conv_taps(
        widen(cot_full),
        jnp.swapaxes(weight_rows, 1, 2),
        planes_local,
        True,
    )
    return (out_acc.astype(jnp.bfloat16), input_acc.astype(jnp.bfloat16), weight_grad)


def solution(mesh):
    split = Mesh(mesh.devices.reshape(mesh.shape["gz"], 2, 2), ("gz", "ch_0", "ch_1"))
    placed = (P(CH, "gz", None, None), P(), P(CH, "gz", None, None))
    return jax.shard_map(
        body,
        mesh=split,
        in_specs=placed,
        out_specs=(P(CH, "gz", None, None), P(CH, "gz", None, None), P(None, "gz", CH)),
        check_vma=False,
    )
```

```python
import math

import jax
import jax.numpy as jnp
from jax import lax
from jax.experimental import pallas as pl
from jax.experimental.pallas import tpu as pltpu
from jax.sharding import Mesh
from jax.sharding import PartitionSpec as P

CH = ("ch_0", "ch_1")
ROW = 128


def padded_2(shard, axis, dim):
    devices, length = (lax.axis_size(axis), shard.shape[dim])
    up = [(i, (i + 1) % devices) for i in range(devices - 1)]
    down = [(j, i) for i, j in up]
    last = lax.slice_in_dim(shard, length - 1, length, axis=dim)
    first = lax.slice_in_dim(shard, 0, 1, axis=dim)
    before = lax.ppermute(last, axis, up)
    after = lax.ppermute(first, axis, down)
    return jnp.concatenate([before, shard, after], axis=dim)


def from_everyone(shard, axis):
    copies = jnp.broadcast_to(shard, (lax.axis_size(axis), *shard.shape))
    return lax.all_to_all(copies, axis, split_axis=0, concat_axis=0, tiled=True)


def summed_on_arrival(shard, axis, dim):
    before, after = (shard.shape[:dim], shard.shape[dim + 1 :])
    devices = lax.axis_size(axis)
    blocks = jnp.moveaxis(shard.reshape(*before, devices, -1, *after), dim, 0)
    arrived = lax.all_to_all(blocks, axis, split_axis=0, concat_axis=0, tiled=True)
    return arrived.astype(jnp.float32).sum(axis=0)

def fused_kernel(g_ref, c_ref, wf_ref, wb_ref, out_ref, ing_ref, wg_ref, vs_ref, cs_ref):
    groups, _, flat = g_ref.shape
    loc = c_ref.shape[0] // 2
    planes = out_ref.shape[0]
    plane = flat // (planes + 2)
    span = (planes - 1) * plane + out_ref.shape[2]
    for k in range(groups):
        vs_ref[k * loc : (k + 1) * loc, :] = g_ref[k, 0:loc, :]
        cs_ref[k * loc : (k + 1) * loc, :] = g_ref[k, loc : 2 * loc, :]
    lane = lax.broadcasted_iota(jnp.int32, (loc, span), 1) % ROW
    first = lane == 0
    last = lane == ROW - 1
    zero = jnp.zeros((loc, span), jnp.float32)
    start = plane + ROW
    cm = c_ref[loc : 2 * loc, start : start + span].astype(jnp.float32)
    c_prev = jnp.where(last, zero, pltpu.roll(cm, span - 1, 1))
    c_next = jnp.where(first, zero, pltpu.roll(cm, 1, 1))
    cstack = jnp.concatenate([c_prev, cm, c_next], axis=0).astype(jnp.bfloat16)

    def shifted_sum(r):
        left = jnp.where(first, zero, pltpu.roll(r[0:loc], 1, 1))
        right = jnp.where(last, zero, pltpu.roll(r[2 * loc : 3 * loc], span - 1, 1))
        return left + r[loc : 2 * loc] + right

    acc_o = zero
    acc_i = zero
    for tap_z in range(3):
        for tap_y in range(3):
            base = tap_z * plane + tap_y * ROW
            pair = 3 * tap_z + tap_y
            sv = vs_ref[:, base : base + span]
            sc = cs_ref[:, base : base + span]
            acc_o = acc_o + shifted_sum(
                jnp.dot(wf_ref[pair], sv, preferred_element_type=jnp.float32)
            )
            acc_i = acc_i + shifted_sum(
                jnp.dot(wb_ref[pair], sc, preferred_element_type=jnp.float32)
            )
            w = lax.dot_general(
                sv, cstack, (((1,), (1,)), ((), ())), preferred_element_type=jnp.float32
            )
            for tap_x in range(3):
                wg_ref[3 * pair + tap_x] = w[:, tap_x * loc : (tap_x + 1) * loc]
    width = out_ref.shape[2]
    for z in range(planes):
        out_ref[z] = acc_o[:, z * plane : z * plane + width].astype(out_ref.dtype)
        ing_ref[z] = acc_i[:, z * plane : z * plane + width].astype(ing_ref.dtype)


def fused(gathered, local, wf, wb, planes, width):
    groups, both, flat = gathered.shape
    loc = both // 2
    cin = groups * loc
    return pl.pallas_call(
        fused_kernel,
        out_shape=(
            jax.ShapeDtypeStruct((planes, loc, width), jnp.bfloat16),
            jax.ShapeDtypeStruct((planes, loc, width), jnp.bfloat16),
            jax.ShapeDtypeStruct((27, cin, loc), jnp.float32),
        ),
        scratch_shapes=[
            pltpu.VMEM((cin, flat), jnp.bfloat16),
            pltpu.VMEM((cin, flat), jnp.bfloat16),
        ],
    )(gathered, local, wf, wb)


def body(volume, weight, cotangent):
    in_local, planes_local, grid_rows, grid_cols = volume.shape
    out_local = cotangent.shape[0]
    my_group = lax.axis_index(CH)
    voxels = planes_local * lax.axis_size("gz") * grid_rows * grid_cols
    both = padded_2(jnp.concatenate([volume, cotangent], axis=0), "gz", 1)
    both = jnp.pad(both, ((0, 0), (0, 0), (1, 1), (0, 0))).reshape(both.shape[0], -1)
    far, near = CH
    blocks = from_everyone(from_everyone(both, far), near)
    gathered = blocks.swapaxes(0, 1).reshape(-1, *both.shape)
    cin = gathered.shape[0] * in_local
    cout = gathered.shape[0] * out_local
    weight_cols = lax.dynamic_slice_in_dim(weight, my_group * out_local, out_local, 2)
    wf = jnp.transpose(weight_cols.reshape(3, 3, 3, cin, out_local), (0, 1, 2, 4, 3))
    wf = wf.reshape(9, 3 * out_local, cin)
    weight_rows = lax.dynamic_slice_in_dim(weight, my_group * in_local, in_local, 1)
    wb = weight_rows[::-1].reshape(9, 3 * in_local, cout)
    out, ing, wg = fused(gathered, both, wf, wb, planes_local, grid_rows * grid_cols)
    shape = (out_local, planes_local, grid_rows, grid_cols)
    out = jnp.transpose(out, (1, 0, 2)).reshape(shape)
    ing = jnp.transpose(ing, (1, 0, 2)).reshape(shape)
    weight_grad = summed_on_arrival(wg.astype(jnp.bfloat16), "gz", 1) * jnp.float32(
        1.0 / math.sqrt(voxels)
    )
    return out, ing, weight_grad


def solution(mesh):
    split = Mesh(mesh.devices.reshape(mesh.shape["gz"], 2, 2), ("gz", "ch_0", "ch_1"))
    placed = (P(CH, "gz", None, None), P(), P(CH, "gz", None, None))
    return jax.shard_map(
        body,
        mesh=split,
        in_specs=placed,
        out_specs=(P(CH, "gz", None, None), P(CH, "gz", None, None), P(None, "gz", CH)),
        check_vma=False,
    )
```

```python
import math

import jax
import jax.numpy as jnp
from jax import lax
from jax.experimental import pallas as pl
from jax.experimental.pallas import tpu as pltpu
from jax.sharding import Mesh
from jax.sharding import PartitionSpec as P

CH = ("ch_0", "ch_1")
ROW = 128


def summed_on_arrival(shard, axis, dim):
    before, after = (shard.shape[:dim], shard.shape[dim + 1 :])
    devices = lax.axis_size(axis)
    blocks = jnp.moveaxis(shard.reshape(*before, devices, -1, *after), dim, 0)
    arrived = lax.all_to_all(blocks, axis, split_axis=0, concat_axis=0, tiled=True)
    return arrived.astype(jnp.float32).sum(axis=0)

def fused_kernel(b_ref, lo_ref, hi_ref, wf_ref, wb_ref, out_ref, ing_ref, wg_ref, vs_ref, cs_ref):
    groups, both, _ = b_ref.shape
    loc = both // 2
    planes, _, width = out_ref.shape
    plane = width + 2 * ROW
    span = (planes - 1) * plane + width
    blank = jnp.zeros((loc, ROW), jnp.bfloat16)
    for k in range(groups):
        rows = slice(k * loc, (k + 1) * loc)
        for ref, low in ((vs_ref, 0), (cs_ref, loc)):
            chans = slice(low, low + loc)
            for zp in range(planes + 2):
                ref[rows, zp * plane : zp * plane + ROW] = blank
                ref[rows, zp * plane + ROW + width : (zp + 1) * plane] = blank
            ref[rows, ROW : ROW + width] = lo_ref[k, chans, :]
            for z in range(planes):
                at = (z + 1) * plane + ROW
                ref[rows, at : at + width] = b_ref[k, chans, z * width : (z + 1) * width]
            at = (planes + 1) * plane + ROW
            ref[rows, at : at + width] = hi_ref[k, chans, :]
    lane = lax.broadcasted_iota(jnp.int32, (loc, span), 1) % ROW
    first = lane == 0
    last = lane == ROW - 1
    zero = jnp.zeros((loc, span), jnp.float32)
    start = plane + ROW
    cm = cs_ref[0:loc, start : start + span].astype(jnp.float32)
    c_prev = jnp.where(last, zero, pltpu.roll(cm, span - 1, 1))
    c_next = jnp.where(first, zero, pltpu.roll(cm, 1, 1))
    cstack = jnp.concatenate([c_prev, cm, c_next], axis=0).astype(jnp.bfloat16)

    def shifted_sum(r):
        left = jnp.where(first, zero, pltpu.roll(r[0:loc], 1, 1))
        right = jnp.where(last, zero, pltpu.roll(r[2 * loc : 3 * loc], span - 1, 1))
        return left + r[loc : 2 * loc] + right

    acc_o = zero
    acc_i = zero
    for tap_z in range(3):
        for tap_y in range(3):
            base = tap_z * plane + tap_y * ROW
            pair = 3 * tap_z + tap_y
            sv = vs_ref[:, base : base + span]
            sc = cs_ref[:, base : base + span]
            acc_o = acc_o + shifted_sum(
                jnp.dot(wf_ref[pair], sv, preferred_element_type=jnp.float32)
            )
            acc_i = acc_i + shifted_sum(
                jnp.dot(wb_ref[pair], sc, preferred_element_type=jnp.float32)
            )
            w = lax.dot_general(
                sv, cstack, (((1,), (1,)), ((), ())), preferred_element_type=jnp.float32
            )
            for tap_x in range(3):
                wg_ref[3 * pair + tap_x] = w[:, tap_x * loc : (tap_x + 1) * loc]
    width = out_ref.shape[2]
    for z in range(planes):
        out_ref[z] = acc_o[:, z * plane : z * plane + width].astype(out_ref.dtype)
        ing_ref[z] = acc_i[:, z * plane : z * plane + width].astype(ing_ref.dtype)


def fused(body, low, high, wf, wb, planes, width):
    groups, both, _ = body.shape
    loc = both // 2
    cin = groups * loc
    flat = (planes + 2) * (width + 2 * ROW)
    return pl.pallas_call(
        fused_kernel,
        out_shape=(
            jax.ShapeDtypeStruct((planes, loc, width), jnp.bfloat16),
            jax.ShapeDtypeStruct((planes, loc, width), jnp.bfloat16),
            jax.ShapeDtypeStruct((27, cin, loc), jnp.float32),
        ),
        scratch_shapes=[
            pltpu.VMEM((cin, flat), jnp.bfloat16),
            pltpu.VMEM((cin, flat), jnp.bfloat16),
        ],
    )(body, low, high, wf, wb)


def by_group(array, order, size, dim):
    return jnp.concatenate(
        [lax.dynamic_slice_in_dim(array, group * size, size, dim) for group in order], axis=dim
    )


def body(volume, weight, cotangent):
    in_local, planes_local, grid_rows, grid_cols = volume.shape
    out_local = cotangent.shape[0]
    my_group = lax.axis_index(CH)
    slabs = lax.axis_size("gz")
    voxels = planes_local * slabs * grid_rows * grid_cols
    width = grid_rows * grid_cols
    both = jnp.concatenate([volume, cotangent], axis=0).reshape(in_local + out_local, -1)
    far, near = CH
    swap = [(0, 1), (1, 0)]
    got_far = lax.ppermute(both, far, swap)
    got_near = lax.ppermute(both, near, swap)
    got_diag = lax.ppermute(got_far, near, swap)
    blocks = jnp.stack([both, got_near, got_far, got_diag])
    groups = blocks.shape[0]
    order = [jnp.bitwise_xor(my_group, j) for j in range(groups)]
    up = [(i, i + 1) for i in range(slabs - 1)]
    down = [(j, i) for i, j in up]
    low = lax.ppermute(blocks[:, :, -width:], "gz", up)
    high = lax.ppermute(blocks[:, :, :width], "gz", down)
    cin = groups * in_local
    cout = groups * out_local
    weight_cols = lax.dynamic_slice_in_dim(weight, my_group * out_local, out_local, 2)
    weight_cols = by_group(weight_cols, order, in_local, 1)
    wf = jnp.transpose(weight_cols.reshape(3, 3, 3, cin, out_local), (0, 1, 2, 4, 3))
    wf = wf.reshape(9, 3 * out_local, cin)
    weight_rows = lax.dynamic_slice_in_dim(weight, my_group * in_local, in_local, 1)
    weight_rows = by_group(weight_rows, order, out_local, 2)
    wb = weight_rows[::-1].reshape(9, 3 * in_local, cout)
    out, ing, wg = fused(blocks, low, high, wf, wb, planes_local, width)
    wg = by_group(wg, order, in_local, 1)
    shape = (out_local, planes_local, grid_rows, grid_cols)
    out = jnp.transpose(out, (1, 0, 2)).reshape(shape)
    ing = jnp.transpose(ing, (1, 0, 2)).reshape(shape)
    weight_grad = summed_on_arrival(wg.astype(jnp.bfloat16), "gz", 1) * jnp.float32(
        1.0 / math.sqrt(voxels)
    )
    return out, ing, weight_grad


def solution(mesh):
    split = Mesh(mesh.devices.reshape(mesh.shape["gz"], 2, 2), ("gz", "ch_0", "ch_1"))
    placed = (P(CH, "gz", None, None), P(), P(CH, "gz", None, None))
    return jax.shard_map(
        body,
        mesh=split,
        in_specs=placed,
        out_specs=(P(CH, "gz", None, None), P(CH, "gz", None, None), P(None, "gz", CH)),
        check_vma=False,
    )
```

```python
import math

import jax
import jax.numpy as jnp
from jax import lax
from jax.experimental import pallas as pl
from jax.experimental.pallas import tpu as pltpu
from jax.sharding import Mesh
from jax.sharding import PartitionSpec as P

CH = ("ch_0", "ch_1")
ROW = 128


def summed_on_arrival(shard, axis, dim):
    before, after = (shard.shape[:dim], shard.shape[dim + 1 :])
    devices = lax.axis_size(axis)
    blocks = jnp.moveaxis(shard.reshape(*before, devices, -1, *after), dim, 0)
    arrived = lax.all_to_all(blocks, axis, split_axis=0, concat_axis=0, tiled=True)
    return arrived.astype(jnp.float32).sum(axis=0)

def fused_kernel(
    own_ref, far_ref, near_ref, lo_ref, hi_ref, flo_ref, fhi_ref, hal_ref, wf_ref, wb_ref,
    out_ref, ing_ref, wg_ref, vs_ref, cs_ref,
):
    both = own_ref.shape[0]
    loc = both // 2
    planes, _, width = out_ref.shape
    plane = width + 2 * ROW
    span = (planes - 1) * plane + width
    blank = jnp.zeros((loc, ROW), jnp.bfloat16)
    pieces = (
        (lambda c: own_ref[c, :], lambda c: lo_ref[c, :], lambda c: hi_ref[c, :]),
        (lambda c: near_ref[0, c, :], lambda c: hal_ref[0, c, :], lambda c: hal_ref[1, c, :]),
        (lambda c: far_ref[c, :], lambda c: flo_ref[c, :], lambda c: fhi_ref[c, :]),
        (lambda c: near_ref[1, c, :], lambda c: hal_ref[2, c, :], lambda c: hal_ref[3, c, :]),
    )
    for k, (body_of, low_of, high_of) in enumerate(pieces):
        rows = slice(k * loc, (k + 1) * loc)
        for ref, low in ((vs_ref, 0), (cs_ref, loc)):
            chans = slice(low, low + loc)
            for zp in range(planes + 2):
                ref[rows, zp * plane : zp * plane + ROW] = blank
                ref[rows, zp * plane + ROW + width : (zp + 1) * plane] = blank
            ref[rows, ROW : ROW + width] = low_of(chans)
            for z in range(planes):
                at = (z + 1) * plane + ROW
                ref[rows, at : at + width] = body_of(chans)[:, z * width : (z + 1) * width]
            at = (planes + 1) * plane + ROW
            ref[rows, at : at + width] = high_of(chans)
    lane = lax.broadcasted_iota(jnp.int32, (loc, span), 1) % ROW
    first = lane == 0
    last = lane == ROW - 1
    zero = jnp.zeros((loc, span), jnp.float32)
    start = plane + ROW
    cm = cs_ref[0:loc, start : start + span].astype(jnp.float32)
    c_prev = jnp.where(last, zero, pltpu.roll(cm, span - 1, 1))
    c_next = jnp.where(first, zero, pltpu.roll(cm, 1, 1))
    cstack = jnp.concatenate([c_prev, cm, c_next], axis=0).astype(jnp.bfloat16)

    def shifted_sum(r):
        left = jnp.where(first, zero, pltpu.roll(r[0:loc], 1, 1))
        right = jnp.where(last, zero, pltpu.roll(r[2 * loc : 3 * loc], span - 1, 1))
        return left + r[loc : 2 * loc] + right

    acc_o = zero
    acc_i = zero
    for tap_z in range(3):
        for tap_y in range(3):
            base = tap_z * plane + tap_y * ROW
            pair = 3 * tap_z + tap_y
            sv = vs_ref[:, base : base + span]
            sc = cs_ref[:, base : base + span]
            acc_o = acc_o + shifted_sum(
                jnp.dot(wf_ref[pair], sv, preferred_element_type=jnp.float32)
            )
            acc_i = acc_i + shifted_sum(
                jnp.dot(wb_ref[pair], sc, preferred_element_type=jnp.float32)
            )
            w = lax.dot_general(
                sv, cstack, (((1,), (1,)), ((), ())), preferred_element_type=jnp.float32
            )
            for tap_x in range(3):
                wg_ref[3 * pair + tap_x] = w[:, tap_x * loc : (tap_x + 1) * loc]
    width = out_ref.shape[2]
    for z in range(planes):
        out_ref[z] = acc_o[:, z * plane : z * plane + width].astype(out_ref.dtype)
        ing_ref[z] = acc_i[:, z * plane : z * plane + width].astype(ing_ref.dtype)


def fused(own, far, near, low, high, far_low, far_high, halos, wf, wb, planes, width):
    both = own.shape[0]
    loc = both // 2
    cin = 4 * loc
    flat = (planes + 2) * (width + 2 * ROW)
    return pl.pallas_call(
        fused_kernel,
        out_shape=(
            jax.ShapeDtypeStruct((planes, loc, width), jnp.bfloat16),
            jax.ShapeDtypeStruct((planes, loc, width), jnp.bfloat16),
            jax.ShapeDtypeStruct((27, cin, loc), jnp.float32),
        ),
        scratch_shapes=[
            pltpu.VMEM((cin, flat), jnp.bfloat16),
            pltpu.VMEM((cin, flat), jnp.bfloat16),
        ],
    )(own, far, near, low, high, far_low, far_high, halos, wf, wb)


def by_group(array, order, size, dim):
    return jnp.concatenate(
        [lax.dynamic_slice_in_dim(array, group * size, size, dim) for group in order], axis=dim
    )


def body(volume, weight, cotangent):
    in_local, planes_local, grid_rows, grid_cols = volume.shape
    out_local = cotangent.shape[0]
    my_group = lax.axis_index(CH)
    slabs = lax.axis_size("gz")
    voxels = planes_local * slabs * grid_rows * grid_cols
    width = grid_rows * grid_cols
    both = jnp.concatenate([volume, cotangent], axis=0).reshape(in_local + out_local, -1)
    far, near = CH
    swap = [(0, 1), (1, 0)]
    up = [(i, i + 1) for i in range(slabs - 1)]
    down = [(j, i) for i, j in up]
    got_far = lax.ppermute(both, far, swap)
    low = lax.ppermute(both[:, -width:], "gz", up)
    high = lax.ppermute(both[:, :width], "gz", down)
    far_low = lax.ppermute(got_far[:, -width:], "gz", up)
    far_high = lax.ppermute(got_far[:, :width], "gz", down)
    got_near = lax.ppermute(jnp.stack([both, got_far]), near, swap)
    halos = lax.ppermute(jnp.stack([low, high, far_low, far_high]), near, swap)
    groups = 4
    order = [jnp.bitwise_xor(my_group, j) for j in range(groups)]
    cin = groups * in_local
    cout = groups * out_local
    weight_cols = lax.dynamic_slice_in_dim(weight, my_group * out_local, out_local, 2)
    weight_cols = by_group(weight_cols, order, in_local, 1)
    wf = jnp.transpose(weight_cols.reshape(3, 3, 3, cin, out_local), (0, 1, 2, 4, 3))
    wf = wf.reshape(9, 3 * out_local, cin)
    weight_rows = lax.dynamic_slice_in_dim(weight, my_group * in_local, in_local, 1)
    weight_rows = by_group(weight_rows, order, out_local, 2)
    wb = weight_rows[::-1].reshape(9, 3 * in_local, cout)
    out, ing, wg = fused(
        both, got_far, got_near, low, high, far_low, far_high, halos, wf, wb, planes_local, width
    )
    wg = by_group(wg, order, in_local, 1)
    shape = (out_local, planes_local, grid_rows, grid_cols)
    out = jnp.transpose(out, (1, 0, 2)).reshape(shape)
    ing = jnp.transpose(ing, (1, 0, 2)).reshape(shape)
    weight_grad = summed_on_arrival(wg.astype(jnp.bfloat16), "gz", 1) * jnp.float32(
        1.0 / math.sqrt(voxels)
    )
    return out, ing, weight_grad


def solution(mesh):
    split = Mesh(mesh.devices.reshape(mesh.shape["gz"], 2, 2), ("gz", "ch_0", "ch_1"))
    placed = (P(CH, "gz", None, None), P(), P(CH, "gz", None, None))
    return jax.shard_map(
        body,
        mesh=split,
        in_specs=placed,
        out_specs=(P(CH, "gz", None, None), P(CH, "gz", None, None), P(None, "gz", CH)),
        check_vma=False,
    )
```

```python
import math

import jax
import jax.numpy as jnp
from jax import lax
from jax.experimental import pallas as pl
from jax.experimental.pallas import tpu as pltpu
from jax.sharding import Mesh
from jax.sharding import PartitionSpec as P

CH = ("ch_0", "ch_1")
GZ = ("gz0", "gz1", "gz2")
ROW = 128


def fused_kernel(
    own_ref, far_ref, near_ref, lo_ref, hi_ref, flo_ref, fhi_ref, hal_ref, wf_ref, wb_ref,
    out_ref, ing_ref, wg_ref, vs_ref, cs_ref,
):
    both = own_ref.shape[0]
    loc = both // 2
    planes, _, width = out_ref.shape
    plane = width + 2 * ROW
    span = (planes - 1) * plane + width
    blank = jnp.zeros((loc, ROW), jnp.bfloat16)
    pieces = (
        (lambda c: own_ref[c, :], lambda c: lo_ref[c, :], lambda c: hi_ref[c, :]),
        (lambda c: near_ref[0, c, :], lambda c: hal_ref[0, c, :], lambda c: hal_ref[1, c, :]),
        (lambda c: far_ref[c, :], lambda c: flo_ref[c, :], lambda c: fhi_ref[c, :]),
        (lambda c: near_ref[1, c, :], lambda c: hal_ref[2, c, :], lambda c: hal_ref[3, c, :]),
    )
    for k, (body_of, low_of, high_of) in enumerate(pieces):
        rows = slice(k * loc, (k + 1) * loc)
        for ref, low in ((vs_ref, 0), (cs_ref, loc)):
            chans = slice(low, low + loc)
            for zp in range(planes + 2):
                ref[rows, zp * plane : zp * plane + ROW] = blank
                ref[rows, zp * plane + ROW + width : (zp + 1) * plane] = blank
            ref[rows, ROW : ROW + width] = low_of(chans)
            for z in range(planes):
                at = (z + 1) * plane + ROW
                ref[rows, at : at + width] = body_of(chans)[:, z * width : (z + 1) * width]
            at = (planes + 1) * plane + ROW
            ref[rows, at : at + width] = high_of(chans)
    lane = lax.broadcasted_iota(jnp.int32, (loc, span), 1) % ROW
    first = lane == 0
    last = lane == ROW - 1
    zero = jnp.zeros((loc, span), jnp.float32)
    start = plane + ROW
    cm = cs_ref[0:loc, start : start + span].astype(jnp.float32)
    c_prev = jnp.where(last, zero, pltpu.roll(cm, span - 1, 1))
    c_next = jnp.where(first, zero, pltpu.roll(cm, 1, 1))
    cstack = jnp.concatenate([c_prev, cm, c_next], axis=0).astype(jnp.bfloat16)

    def shifted_sum(r):
        left = jnp.where(first, zero, pltpu.roll(r[0:loc], 1, 1))
        right = jnp.where(last, zero, pltpu.roll(r[2 * loc : 3 * loc], span - 1, 1))
        return left + r[loc : 2 * loc] + right

    acc_o = zero
    acc_i = zero
    for tap_z in range(3):
        for tap_y in range(3):
            base = tap_z * plane + tap_y * ROW
            pair = 3 * tap_z + tap_y
            sv = vs_ref[:, base : base + span]
            sc = cs_ref[:, base : base + span]
            acc_o = acc_o + shifted_sum(
                jnp.dot(wf_ref[pair], sv, preferred_element_type=jnp.float32)
            )
            acc_i = acc_i + shifted_sum(
                jnp.dot(wb_ref[pair], sc, preferred_element_type=jnp.float32)
            )
            w = lax.dot_general(
                sv, cstack, (((1,), (1,)), ((), ())), preferred_element_type=jnp.float32
            )
            for tap_x in range(3):
                wg_ref[3 * pair + tap_x] = w[:, tap_x * loc : (tap_x + 1) * loc]
    width = out_ref.shape[2]
    for z in range(planes):
        out_ref[z] = acc_o[:, z * plane : z * plane + width].astype(out_ref.dtype)
        ing_ref[z] = acc_i[:, z * plane : z * plane + width].astype(ing_ref.dtype)


def fused(own, far, near, low, high, far_low, far_high, halos, wf, wb, planes, width):
    both = own.shape[0]
    loc = both // 2
    cin = 4 * loc
    flat = (planes + 2) * (width + 2 * ROW)
    return pl.pallas_call(
        fused_kernel,
        out_shape=(
            jax.ShapeDtypeStruct((planes, loc, width), jnp.bfloat16),
            jax.ShapeDtypeStruct((planes, loc, width), jnp.bfloat16),
            jax.ShapeDtypeStruct((27, cin, loc), jnp.float32),
        ),
        scratch_shapes=[
            pltpu.VMEM((cin, flat), jnp.bfloat16),
            pltpu.VMEM((cin, flat), jnp.bfloat16),
        ],
    )(own, far, near, low, high, far_low, far_high, halos, wf, wb)


def by_group(array, order, size, dim):
    return jnp.concatenate(
        [lax.dynamic_slice_in_dim(array, group * size, size, dim) for group in order], axis=dim
    )


def body(volume, weight, cotangent):
    in_local, planes_local, grid_rows, grid_cols = volume.shape
    out_local = cotangent.shape[0]
    my_group = lax.axis_index(CH)
    slabs = lax.axis_size(GZ)
    voxels = planes_local * slabs * grid_rows * grid_cols
    width = grid_rows * grid_cols
    both = jnp.concatenate([volume, cotangent], axis=0).reshape(in_local + out_local, -1)
    far, near = CH
    swap = [(0, 1), (1, 0)]
    up = [(i, i + 1) for i in range(slabs - 1)]
    down = [(j, i) for i, j in up]
    got_far = lax.ppermute(both, far, swap)
    low = lax.ppermute(both[:, -width:], GZ, up)
    high = lax.ppermute(both[:, :width], GZ, down)
    far_low = lax.ppermute(got_far[:, -width:], GZ, up)
    far_high = lax.ppermute(got_far[:, :width], GZ, down)
    got_near = lax.ppermute(jnp.stack([both, got_far]), near, swap)
    halos = lax.ppermute(jnp.stack([low, high, far_low, far_high]), near, swap)
    groups = 4
    order = [jnp.bitwise_xor(my_group, j) for j in range(groups)]
    cin = groups * in_local
    cout = groups * out_local
    weight_cols = lax.dynamic_slice_in_dim(weight, my_group * out_local, out_local, 2)
    weight_cols = by_group(weight_cols, order, in_local, 1)
    wf = jnp.transpose(weight_cols.reshape(3, 3, 3, cin, out_local), (0, 1, 2, 4, 3))
    wf = wf.reshape(9, 3 * out_local, cin)
    weight_rows = lax.dynamic_slice_in_dim(weight, my_group * in_local, in_local, 1)
    weight_rows = by_group(weight_rows, order, out_local, 2)
    wb = weight_rows[::-1].reshape(9, 3 * in_local, cout)
    out, ing, wg = fused(
        both, got_far, got_near, low, high, far_low, far_high, halos, wf, wb, planes_local, width
    )
    wg = by_group(wg, order, in_local, 1)
    shape = (out_local, planes_local, grid_rows, grid_cols)
    out = jnp.transpose(out, (1, 0, 2)).reshape(shape)
    ing = jnp.transpose(ing, (1, 0, 2)).reshape(shape)
    rows = [mesh_size for mesh_size in (lax.axis_size(GZ[0]), lax.axis_size(GZ[1]), lax.axis_size(GZ[2]))]
    part = wg.astype(jnp.bfloat16).reshape(27, rows[0] * rows[1], rows[2], -1, out_local)
    part = jnp.moveaxis(part, 2, 0)
    part = lax.all_to_all(part, GZ[2], split_axis=0, concat_axis=0, tiled=True)
    part = jnp.moveaxis(part.astype(jnp.float32).sum(axis=0), 1, 0)
    part = lax.all_to_all(part, GZ[:2], split_axis=0, concat_axis=0, tiled=True)
    weight_grad = part.sum(axis=0) * jnp.float32(1.0 / math.sqrt(voxels))
    return out, ing, weight_grad


def solution(mesh):
    plan = dict(mesh.shape)
    sizes = (2, 4, plan["gz"] // 8, 2, plan["ch"] // 2)
    split = Mesh(mesh.devices.reshape(sizes), GZ + CH)
    placed = (P(CH, GZ, None, None), P(), P(CH, GZ, None, None))
    return jax.shard_map(
        body,
        mesh=split,
        in_specs=placed,
        out_specs=(P(CH, GZ, None, None), P(CH, GZ, None, None), P(None, GZ, CH)),
        check_vma=False,
    )
```

```python
import math

import jax
import jax.numpy as jnp
from jax import lax
from jax.experimental import pallas as pl
from jax.experimental.pallas import tpu as pltpu
from jax.sharding import Mesh
from jax.sharding import PartitionSpec as P

CH = ("ch_0", "ch_1")
ROW = 128


def summed_on_arrival(shard, axis, dim):
    before, after = (shard.shape[:dim], shard.shape[dim + 1 :])
    devices = lax.axis_size(axis)
    blocks = jnp.moveaxis(shard.reshape(*before, devices, -1, *after), dim, 0)
    arrived = lax.all_to_all(blocks, axis, split_axis=0, concat_axis=0, tiled=True)
    return arrived.astype(jnp.float32).sum(axis=0)

def fused_kernel(
    own_ref, far_ref, near_ref, lo_ref, hi_ref, flo_ref, fhi_ref, hal_ref, wf_ref, wb_ref,
    out_ref, ing_ref, wg_ref, vs_ref, cs_ref,
):
    both = own_ref.shape[0]
    loc = both // 2
    planes, _, width = out_ref.shape
    plane = width + 2 * ROW
    span = (planes - 1) * plane + width
    blank = jnp.zeros((loc, ROW), jnp.bfloat16)
    pieces = (
        (lambda c: own_ref[c, :], lambda c: lo_ref[c, :], lambda c: hi_ref[c, :]),
        (lambda c: near_ref[0, c, :], lambda c: hal_ref[0, c, :], lambda c: hal_ref[1, c, :]),
        (lambda c: far_ref[c, :], lambda c: flo_ref[c, :], lambda c: fhi_ref[c, :]),
        (lambda c: near_ref[1, c, :], lambda c: hal_ref[2, c, :], lambda c: hal_ref[3, c, :]),
    )
    for k, (body_of, low_of, high_of) in enumerate(pieces):
        rows = slice(k * loc, (k + 1) * loc)
        for ref, low in ((vs_ref, 0), (cs_ref, loc)):
            chans = slice(low, low + loc)
            for zp in range(planes + 2):
                ref[rows, zp * plane : zp * plane + ROW] = blank
                ref[rows, zp * plane + ROW + width : (zp + 1) * plane] = blank
            ref[rows, ROW : ROW + width] = low_of(chans)
            for z in range(planes):
                at = (z + 1) * plane + ROW
                ref[rows, at : at + width] = body_of(chans)[:, z * width : (z + 1) * width]
            at = (planes + 1) * plane + ROW
            ref[rows, at : at + width] = high_of(chans)
    lane = lax.broadcasted_iota(jnp.int32, (loc, span), 1) % ROW
    first = lane == 0
    last = lane == ROW - 1
    zero = jnp.zeros((loc, span), jnp.float32)
    start = plane + ROW
    cm = cs_ref[0:loc, start : start + span].astype(jnp.float32)
    c_prev = jnp.where(last, zero, pltpu.roll(cm, span - 1, 1))
    c_next = jnp.where(first, zero, pltpu.roll(cm, 1, 1))
    cstack = jnp.concatenate([c_prev, cm, c_next], axis=0).astype(jnp.bfloat16)

    def shifted_sum(r):
        left = jnp.where(first, zero, pltpu.roll(r[0:loc], 1, 1))
        right = jnp.where(last, zero, pltpu.roll(r[2 * loc : 3 * loc], span - 1, 1))
        return left + r[loc : 2 * loc] + right

    acc_o = zero
    acc_i = zero
    for tap_z in range(3):
        for tap_y in range(3):
            base = tap_z * plane + tap_y * ROW
            pair = 3 * tap_z + tap_y
            sv = vs_ref[:, base : base + span]
            sc = cs_ref[:, base : base + span]
            acc_o = acc_o + shifted_sum(
                jnp.dot(wf_ref[pair], sv, preferred_element_type=jnp.float32)
            )
            acc_i = acc_i + shifted_sum(
                jnp.dot(wb_ref[pair], sc, preferred_element_type=jnp.float32)
            )
            w = lax.dot_general(
                sv, cstack, (((1,), (1,)), ((), ())), preferred_element_type=jnp.float32
            )
            for tap_x in range(3):
                wg_ref[3 * pair + tap_x] = w[:, tap_x * loc : (tap_x + 1) * loc]
    width = out_ref.shape[2]
    for z in range(planes):
        out_ref[z] = acc_o[:, z * plane : z * plane + width].astype(out_ref.dtype)
        ing_ref[z] = acc_i[:, z * plane : z * plane + width].astype(ing_ref.dtype)


def fused(own, far, near, low, high, far_low, far_high, halos, wf, wb, planes, width):
    both = own.shape[0]
    loc = both // 2
    cin = 4 * loc
    flat = (planes + 2) * (width + 2 * ROW)
    return pl.pallas_call(
        fused_kernel,
        out_shape=(
            jax.ShapeDtypeStruct((planes, loc, width), jnp.bfloat16),
            jax.ShapeDtypeStruct((planes, loc, width), jnp.bfloat16),
            jax.ShapeDtypeStruct((27, cin, loc), jnp.float32),
        ),
        scratch_shapes=[
            pltpu.VMEM((cin, flat), jnp.bfloat16),
            pltpu.VMEM((cin, flat), jnp.bfloat16),
        ],
    )(own, far, near, low, high, far_low, far_high, halos, wf, wb)


def by_group(array, order, size, dim):
    return jnp.concatenate(
        [lax.dynamic_slice_in_dim(array, group * size, size, dim) for group in order], axis=dim
    )


def body(volume, weight, cotangent):
    in_local, planes_local, grid_rows, grid_cols = volume.shape
    out_local = cotangent.shape[0]
    my_group = lax.axis_index(CH)
    slabs = lax.axis_size("gz")
    voxels = planes_local * slabs * grid_rows * grid_cols
    width = grid_rows * grid_cols
    both = jnp.concatenate([volume, cotangent], axis=0).reshape(in_local + out_local, -1)
    far, near = CH
    swap = [(0, 1), (1, 0)]
    up = [(i, i + 1) for i in range(slabs - 1)]
    down = [(j, i) for i, j in up]
    got_far = lax.ppermute(both, far, swap)
    low = lax.ppermute(both[:, -width:], "gz", up)
    high = lax.ppermute(both[:, :width], "gz", down)
    groups = 4
    order = [jnp.bitwise_xor(my_group, j) for j in range(groups)]
    cin = groups * in_local
    cout = groups * out_local
    weight_cols = lax.dynamic_slice_in_dim(weight, my_group * out_local, out_local, 2)
    weight_cols = by_group(weight_cols, order, in_local, 1)
    wf = jnp.transpose(weight_cols.reshape(3, 3, 3, cin, out_local), (0, 1, 2, 4, 3))
    wf = wf.reshape(9, 3 * out_local, cin)
    weight_rows = lax.dynamic_slice_in_dim(weight, my_group * in_local, in_local, 1)
    weight_rows = by_group(weight_rows, order, out_local, 2)
    wb = weight_rows[::-1].reshape(9, 3 * in_local, cout)
    got_far, wf, wb = lax.optimization_barrier((got_far, wf, wb))
    far_low = lax.ppermute(got_far[:, -width:], "gz", up)
    far_high = lax.ppermute(got_far[:, :width], "gz", down)
    got_near = lax.ppermute(jnp.stack([both, got_far]), near, swap)
    halos = lax.ppermute(jnp.stack([low, high, far_low, far_high]), near, swap)
    out, ing, wg = fused(
        both, got_far, got_near, low, high, far_low, far_high, halos, wf, wb, planes_local, width
    )
    wg = by_group(wg, order, in_local, 1)
    shape = (out_local, planes_local, grid_rows, grid_cols)
    out = jnp.transpose(out, (1, 0, 2)).reshape(shape)
    ing = jnp.transpose(ing, (1, 0, 2)).reshape(shape)
    weight_grad = summed_on_arrival(wg.astype(jnp.bfloat16), "gz", 1) * jnp.float32(
        1.0 / math.sqrt(voxels)
    )
    return out, ing, weight_grad


def solution(mesh):
    split = Mesh(mesh.devices.reshape(mesh.shape["gz"], 2, 2), ("gz", "ch_0", "ch_1"))
    placed = (P(CH, "gz", None, None), P(), P(CH, "gz", None, None))
    return jax.shard_map(
        body,
        mesh=split,
        in_specs=placed,
        out_specs=(P(CH, "gz", None, None), P(CH, "gz", None, None), P(None, "gz", CH)),
        check_vma=False,
    )
```

```python
import math

import jax
import jax.numpy as jnp
from jax import lax
from jax.experimental import pallas as pl
from jax.experimental.pallas import tpu as pltpu
from jax.sharding import Mesh
from jax.sharding import PartitionSpec as P

CH = ("ch_0", "ch_1")
ROW = 128


def summed_on_arrival(shard, axis, dim):
    before, after = (shard.shape[:dim], shard.shape[dim + 1 :])
    devices = lax.axis_size(axis)
    blocks = jnp.moveaxis(shard.reshape(*before, devices, -1, *after), dim, 0)
    arrived = lax.all_to_all(blocks, axis, split_axis=0, concat_axis=0, tiled=True)
    return arrived.astype(jnp.float32).sum(axis=0)

def fused_kernel(
    own_ref, far_ref, near_ref, lo_ref, hi_ref, flo_ref, fhi_ref, hal_ref, wf_ref, wb_ref,
    out_ref, ing_ref, wg_ref, vs_ref, cs_ref, *, grads,
):
    both = own_ref.shape[0]
    loc = both // 2
    width = lo_ref.shape[1]
    planes = own_ref.shape[1] // width
    plane = width + 2 * ROW
    span = (planes - 1) * plane + width
    blank = jnp.zeros((loc, ROW), jnp.bfloat16)
    pieces = (
        (lambda c: own_ref[c, :], lambda c: lo_ref[c, :], lambda c: hi_ref[c, :]),
        (lambda c: near_ref[0, c, :], lambda c: hal_ref[0, c, :], lambda c: hal_ref[1, c, :]),
        (lambda c: far_ref[c, :], lambda c: flo_ref[c, :], lambda c: fhi_ref[c, :]),
        (lambda c: near_ref[1, c, :], lambda c: hal_ref[2, c, :], lambda c: hal_ref[3, c, :]),
    )
    for k, (body_of, low_of, high_of) in enumerate(pieces):
        rows = slice(k * loc, (k + 1) * loc)
        targets = ((vs_ref, 0), (cs_ref, loc)) if (not grads or k == 0) else ((vs_ref, 0),)
        for ref, low in targets:
            chans = slice(low, low + loc)
            for zp in range(planes + 2):
                ref[rows, zp * plane : zp * plane + ROW] = blank
                ref[rows, zp * plane + ROW + width : (zp + 1) * plane] = blank
            ref[rows, ROW : ROW + width] = low_of(chans)
            for z in range(planes):
                at = (z + 1) * plane + ROW
                ref[rows, at : at + width] = body_of(chans)[:, z * width : (z + 1) * width]
            at = (planes + 1) * plane + ROW
            ref[rows, at : at + width] = high_of(chans)
    lane = lax.broadcasted_iota(jnp.int32, (loc, span), 1) % ROW
    first = lane == 0
    last = lane == ROW - 1
    zero = jnp.zeros((loc, span), jnp.float32)
    if grads:
        start = plane + ROW
        cm = cs_ref[0:loc, start : start + span].astype(jnp.float32)
        c_prev = jnp.where(last, zero, pltpu.roll(cm, span - 1, 1))
        c_next = jnp.where(first, zero, pltpu.roll(cm, 1, 1))
        cstack = jnp.concatenate([c_prev, cm, c_next], axis=0).astype(jnp.bfloat16)

    def shifted_sum(r):
        left = jnp.where(first, zero, pltpu.roll(r[0:loc], 1, 1))
        right = jnp.where(last, zero, pltpu.roll(r[2 * loc : 3 * loc], span - 1, 1))
        return left + r[loc : 2 * loc] + right

    acc_o = zero
    acc_i = zero
    for tap_z in range(3):
        for tap_y in range(3):
            base = tap_z * plane + tap_y * ROW
            pair = 3 * tap_z + tap_y
            sv = vs_ref[:, base : base + span]
            if grads:
                w = lax.dot_general(
                    sv, cstack, (((1,), (1,)), ((), ())), preferred_element_type=jnp.float32
                )
                for tap_x in range(3):
                    wg_ref[3 * pair + tap_x] = w[:, tap_x * loc : (tap_x + 1) * loc]
                continue
            sc = cs_ref[:, base : base + span]
            acc_o = acc_o + shifted_sum(
                jnp.dot(wf_ref[pair], sv, preferred_element_type=jnp.float32)
            )
            acc_i = acc_i + shifted_sum(
                jnp.dot(wb_ref[pair], sc, preferred_element_type=jnp.float32)
            )
    if grads:
        return
    width = out_ref.shape[2]
    for z in range(planes):
        out_ref[z] = acc_o[:, z * plane : z * plane + width].astype(out_ref.dtype)
        ing_ref[z] = acc_i[:, z * plane : z * plane + width].astype(ing_ref.dtype)


def fused(pieces, wf, wb, planes, width, grads):
    both = pieces[0].shape[0]
    loc = both // 2
    cin = 4 * loc
    flat = (planes + 2) * (width + 2 * ROW)
    if grads:
        shapes = (jax.ShapeDtypeStruct((27, cin, loc), jnp.float32),)
    else:
        shapes = (
            jax.ShapeDtypeStruct((planes, loc, width), jnp.bfloat16),
            jax.ShapeDtypeStruct((planes, loc, width), jnp.bfloat16),
        )

    def kernel(*refs):
        ins = refs[:10]
        outs = refs[10:-2]
        scratch = refs[-2:]
        if grads:
            outs = (None, None) + tuple(outs)
        else:
            outs = tuple(outs) + (None,)
        fused_kernel(*ins, *outs, *scratch, grads=grads)

    return pl.pallas_call(
        kernel,
        out_shape=shapes,
        scratch_shapes=[
            pltpu.VMEM((cin, flat), jnp.bfloat16),
            pltpu.VMEM((cin, flat), jnp.bfloat16),
        ],
    )(*pieces, wf, wb)


def by_group(array, order, size, dim):
    return jnp.concatenate(
        [lax.dynamic_slice_in_dim(array, group * size, size, dim) for group in order], axis=dim
    )


def body(volume, weight, cotangent):
    in_local, planes_local, grid_rows, grid_cols = volume.shape
    out_local = cotangent.shape[0]
    my_group = lax.axis_index(CH)
    slabs = lax.axis_size("gz")
    voxels = planes_local * slabs * grid_rows * grid_cols
    width = grid_rows * grid_cols
    both = jnp.concatenate([volume, cotangent], axis=0).reshape(in_local + out_local, -1)
    far, near = CH
    swap = [(0, 1), (1, 0)]
    up = [(i, i + 1) for i in range(slabs - 1)]
    down = [(j, i) for i, j in up]
    got_far = lax.ppermute(both, far, swap)
    low = lax.ppermute(both[:, -width:], "gz", up)
    high = lax.ppermute(both[:, :width], "gz", down)
    far_low = lax.ppermute(got_far[:, -width:], "gz", up)
    far_high = lax.ppermute(got_far[:, :width], "gz", down)
    got_near = lax.ppermute(jnp.stack([both, got_far]), near, swap)
    halos = lax.ppermute(jnp.stack([low, high, far_low, far_high]), near, swap)
    groups = 4
    order = [jnp.bitwise_xor(my_group, j) for j in range(groups)]
    cin = groups * in_local
    cout = groups * out_local
    weight_cols = lax.dynamic_slice_in_dim(weight, my_group * out_local, out_local, 2)
    weight_cols = by_group(weight_cols, order, in_local, 1)
    wf = jnp.transpose(weight_cols.reshape(3, 3, 3, cin, out_local), (0, 1, 2, 4, 3))
    wf = wf.reshape(9, 3 * out_local, cin)
    weight_rows = lax.dynamic_slice_in_dim(weight, my_group * in_local, in_local, 1)
    weight_rows = by_group(weight_rows, order, out_local, 2)
    wb = weight_rows[::-1].reshape(9, 3 * in_local, cout)
    pieces = (both, got_far, got_near, low, high, far_low, far_high, halos)
    (wg,) = fused(pieces, wf, wb, planes_local, width, True)
    wg = by_group(wg, order, in_local, 1)
    out, ing = fused(pieces, wf, wb, planes_local, width, False)
    shape = (out_local, planes_local, grid_rows, grid_cols)
    out = jnp.transpose(out, (1, 0, 2)).reshape(shape)
    ing = jnp.transpose(ing, (1, 0, 2)).reshape(shape)
    weight_grad = summed_on_arrival(wg.astype(jnp.bfloat16), "gz", 1) * jnp.float32(
        1.0 / math.sqrt(voxels)
    )
    return out, ing, weight_grad


def solution(mesh):
    split = Mesh(mesh.devices.reshape(mesh.shape["gz"], 2, 2), ("gz", "ch_0", "ch_1"))
    placed = (P(CH, "gz", None, None), P(), P(CH, "gz", None, None))
    return jax.shard_map(
        body,
        mesh=split,
        in_specs=placed,
        out_specs=(P(CH, "gz", None, None), P(CH, "gz", None, None), P(None, "gz", CH)),
        check_vma=False,
    )
```

```python
import math

import jax
import jax.numpy as jnp
from jax import lax
from jax.experimental import pallas as pl
from jax.experimental.pallas import tpu as pltpu
from jax.sharding import Mesh
from jax.sharding import PartitionSpec as P

CH = ("ch_0", "ch_1")
ROW = 128


def summed_on_arrival(shard, axis, dim):
    before, after = (shard.shape[:dim], shard.shape[dim + 1 :])
    devices = lax.axis_size(axis)
    blocks = jnp.moveaxis(shard.reshape(*before, devices, -1, *after), dim, 0)
    arrived = lax.all_to_all(blocks, axis, split_axis=0, concat_axis=0, tiled=True)
    return arrived.astype(jnp.float32).sum(axis=0)

def fused_kernel(
    own_ref, far_ref, near_ref, lo_ref, hi_ref, flo_ref, fhi_ref, hal_ref, wf_ref, wb_ref,
    out_ref, ing_ref, wg_ref, vs_ref, cs_ref, *, grads,
):
    both = own_ref.shape[0]
    loc = both // 2
    width = lo_ref.shape[1]
    planes = own_ref.shape[1] // width
    plane = width + 2 * ROW
    span = (planes - 1) * plane + width
    blank = jnp.zeros((loc, ROW), jnp.bfloat16)
    pieces = (
        (lambda c: own_ref[c, :], lambda c: lo_ref[c, :], lambda c: hi_ref[c, :]),
        (lambda c: near_ref[0, c, :], lambda c: hal_ref[0, c, :], lambda c: hal_ref[1, c, :]),
        (lambda c: far_ref[c, :], lambda c: flo_ref[c, :], lambda c: fhi_ref[c, :]),
        (lambda c: near_ref[1, c, :], lambda c: hal_ref[2, c, :], lambda c: hal_ref[3, c, :]),
    )
    for k, (body_of, low_of, high_of) in enumerate(pieces):
        rows = slice(k * loc, (k + 1) * loc)
        targets = ((vs_ref, 0), (cs_ref, loc)) if (not grads or k == 0) else ((vs_ref, 0),)
        for ref, low in targets:
            chans = slice(low, low + loc)
            for zp in range(planes + 2):
                ref[rows, zp * plane : zp * plane + ROW] = blank
                ref[rows, zp * plane + ROW + width : (zp + 1) * plane] = blank
            ref[rows, ROW : ROW + width] = low_of(chans)
            for z in range(planes):
                at = (z + 1) * plane + ROW
                ref[rows, at : at + width] = body_of(chans)[:, z * width : (z + 1) * width]
            at = (planes + 1) * plane + ROW
            ref[rows, at : at + width] = high_of(chans)
    lane = lax.broadcasted_iota(jnp.int32, (loc, span), 1) % ROW
    first = lane == 0
    last = lane == ROW - 1
    zero = jnp.zeros((loc, span), jnp.float32)
    if grads:
        start = plane + ROW
        cm = cs_ref[0:loc, start : start + span].astype(jnp.float32)
        c_prev = jnp.where(last, zero, pltpu.roll(cm, span - 1, 1))
        c_next = jnp.where(first, zero, pltpu.roll(cm, 1, 1))
        cstack = jnp.concatenate([c_prev, cm, c_next], axis=0).astype(jnp.bfloat16)

    def shifted_sum(r):
        left = jnp.where(first, zero, pltpu.roll(r[0:loc], 1, 1))
        right = jnp.where(last, zero, pltpu.roll(r[2 * loc : 3 * loc], span - 1, 1))
        return left + r[loc : 2 * loc] + right

    acc_o = zero
    acc_i = zero
    for tap_z in range(3):
        for tap_y in range(3):
            base = tap_z * plane + tap_y * ROW
            pair = 3 * tap_z + tap_y
            sv = vs_ref[:, base : base + span]
            if grads:
                w = lax.dot_general(
                    sv, cstack, (((1,), (1,)), ((), ())), preferred_element_type=jnp.float32
                )
                for tap_x in range(3):
                    wg_ref[3 * pair + tap_x] = w[:, tap_x * loc : (tap_x + 1) * loc]
                continue
            sc = cs_ref[:, base : base + span]
            acc_o = acc_o + shifted_sum(
                jnp.dot(wf_ref[pair], sv, preferred_element_type=jnp.float32)
            )
            acc_i = acc_i + shifted_sum(
                jnp.dot(wb_ref[pair], sc, preferred_element_type=jnp.float32)
            )
    if grads:
        return
    width = out_ref.shape[2]
    for z in range(planes):
        out_ref[z] = acc_o[:, z * plane : z * plane + width].astype(out_ref.dtype)
        ing_ref[z] = acc_i[:, z * plane : z * plane + width].astype(ing_ref.dtype)


def fused(pieces, wf, wb, planes, width, grads):
    both = pieces[0].shape[0]
    loc = both // 2
    cin = 4 * loc
    flat = (planes + 2) * (width + 2 * ROW)
    if grads:
        shapes = (jax.ShapeDtypeStruct((27, cin, loc), jnp.float32),)
    else:
        shapes = (
            jax.ShapeDtypeStruct((planes, loc, width), jnp.bfloat16),
            jax.ShapeDtypeStruct((planes, loc, width), jnp.bfloat16),
        )

    def kernel(*refs):
        ins = refs[:10]
        outs = refs[10:-2]
        scratch = refs[-2:]
        if grads:
            outs = (None, None) + tuple(outs)
        else:
            outs = tuple(outs) + (None,)
        fused_kernel(*ins, *outs, *scratch, grads=grads)

    return pl.pallas_call(
        kernel,
        out_shape=shapes,
        scratch_shapes=[
            pltpu.VMEM((cin, flat), jnp.bfloat16),
            pltpu.VMEM((cin, flat), jnp.bfloat16),
        ],
    )(*pieces, wf, wb)


def by_group(array, order, size, dim):
    return jnp.concatenate(
        [lax.dynamic_slice_in_dim(array, group * size, size, dim) for group in order], axis=dim
    )


def body(volume, weight, cotangent):
    in_local, planes_local, grid_rows, grid_cols = volume.shape
    out_local = cotangent.shape[0]
    my_group = lax.axis_index(CH)
    slabs = lax.axis_size("gz")
    voxels = planes_local * slabs * grid_rows * grid_cols
    width = grid_rows * grid_cols
    both = jnp.concatenate([volume, cotangent], axis=0).reshape(in_local + out_local, -1)
    far, near = CH
    swap = [(0, 1), (1, 0)]
    up = [(i, i + 1) for i in range(slabs - 1)]
    down = [(j, i) for i, j in up]
    got_far = lax.ppermute(both, far, swap)
    low = lax.ppermute(both[:, -width:], "gz", up)
    high = lax.ppermute(both[:, :width], "gz", down)
    groups = 4
    order = [jnp.bitwise_xor(my_group, j) for j in range(groups)]
    cin = groups * in_local
    cout = groups * out_local
    weight_cols = lax.dynamic_slice_in_dim(weight, my_group * out_local, out_local, 2)
    weight_cols = by_group(weight_cols, order, in_local, 1)
    wf = jnp.transpose(weight_cols.reshape(3, 3, 3, cin, out_local), (0, 1, 2, 4, 3))
    wf = wf.reshape(9, 3 * out_local, cin)
    weight_rows = lax.dynamic_slice_in_dim(weight, my_group * in_local, in_local, 1)
    weight_rows = by_group(weight_rows, order, out_local, 2)
    wb = weight_rows[::-1].reshape(9, 3 * in_local, cout)
    got_far, wf, wb = lax.optimization_barrier((got_far, wf, wb))
    far_low = lax.ppermute(got_far[:, -width:], "gz", up)
    far_high = lax.ppermute(got_far[:, :width], "gz", down)
    got_near = lax.ppermute(jnp.stack([both, got_far]), near, swap)
    halos = lax.ppermute(jnp.stack([low, high, far_low, far_high]), near, swap)
    pieces = (both, got_far, got_near, low, high, far_low, far_high, halos)
    (wg,) = fused(pieces, wf, wb, planes_local, width, True)
    wg = by_group(wg, order, in_local, 1)
    out, ing = fused(pieces, wf, wb, planes_local, width, False)
    shape = (out_local, planes_local, grid_rows, grid_cols)
    out = jnp.transpose(out, (1, 0, 2)).reshape(shape)
    ing = jnp.transpose(ing, (1, 0, 2)).reshape(shape)
    weight_grad = summed_on_arrival(wg.astype(jnp.bfloat16), "gz", 1) * jnp.float32(
        1.0 / math.sqrt(voxels)
    )
    return out, ing, weight_grad


def solution(mesh):
    split = Mesh(mesh.devices.reshape(mesh.shape["gz"], 2, 2), ("gz", "ch_0", "ch_1"))
    placed = (P(CH, "gz", None, None), P(), P(CH, "gz", None, None))
    return jax.shard_map(
        body,
        mesh=split,
        in_specs=placed,
        out_specs=(P(CH, "gz", None, None), P(CH, "gz", None, None), P(None, "gz", CH)),
        check_vma=False,
    )
```

```python
import math

import jax
import jax.numpy as jnp
from jax import lax
from jax.experimental import pallas as pl
from jax.experimental.pallas import tpu as pltpu
from jax.sharding import Mesh
from jax.sharding import PartitionSpec as P

CH = ("ch_0", "ch_1")
ROW = 128


def summed_on_arrival(shard, axis, dim):
    before, after = (shard.shape[:dim], shard.shape[dim + 1 :])
    devices = lax.axis_size(axis)
    blocks = jnp.moveaxis(shard.reshape(*before, devices, -1, *after), dim, 0)
    arrived = lax.all_to_all(blocks, axis, split_axis=0, concat_axis=0, tiled=True)
    return arrived.astype(jnp.float32).sum(axis=0)

def fused_kernel(
    own_ref, far_ref, near_ref, lo_ref, hi_ref, flo_ref, fhi_ref, hal_ref, wf_ref, wb_ref,
    out_ref, ing_ref, wg_ref, vs_ref, cs_ref,
):
    both = own_ref.shape[0]
    loc = both // 2
    planes = out_ref.shape[1]
    width = out_ref.shape[2] * out_ref.shape[3]
    plane = width + 2 * ROW
    span = (planes - 1) * plane + width
    blank = jnp.zeros((loc, ROW), jnp.bfloat16)
    pieces = (
        (lambda c: own_ref[c, :], lambda c: lo_ref[c, :], lambda c: hi_ref[c, :]),
        (lambda c: near_ref[0, c, :], lambda c: hal_ref[0, c, :], lambda c: hal_ref[1, c, :]),
        (lambda c: far_ref[c, :], lambda c: flo_ref[c, :], lambda c: fhi_ref[c, :]),
        (lambda c: near_ref[1, c, :], lambda c: hal_ref[2, c, :], lambda c: hal_ref[3, c, :]),
    )
    for k, (body_of, low_of, high_of) in enumerate(pieces):
        rows = slice(k * loc, (k + 1) * loc)
        for ref, low in ((vs_ref, 0), (cs_ref, loc)):
            chans = slice(low, low + loc)
            for zp in range(planes + 2):
                ref[rows, zp * plane : zp * plane + ROW] = blank
                ref[rows, zp * plane + ROW + width : (zp + 1) * plane] = blank
            ref[rows, ROW : ROW + width] = low_of(chans)
            for z in range(planes):
                at = (z + 1) * plane + ROW
                ref[rows, at : at + width] = body_of(chans)[:, z * width : (z + 1) * width]
            at = (planes + 1) * plane + ROW
            ref[rows, at : at + width] = high_of(chans)
    lane = lax.broadcasted_iota(jnp.int32, (loc, span), 1) % ROW
    first = lane == 0
    last = lane == ROW - 1
    zero = jnp.zeros((loc, span), jnp.float32)
    start = plane + ROW
    cm = cs_ref[0:loc, start : start + span].astype(jnp.float32)
    c_prev = jnp.where(last, zero, pltpu.roll(cm, span - 1, 1))
    c_next = jnp.where(first, zero, pltpu.roll(cm, 1, 1))
    cstack = jnp.concatenate([c_prev, cm, c_next], axis=0).astype(jnp.bfloat16)

    def shifted_sum(r):
        left = jnp.where(first, zero, pltpu.roll(r[0:loc], 1, 1))
        right = jnp.where(last, zero, pltpu.roll(r[2 * loc : 3 * loc], span - 1, 1))
        return left + r[loc : 2 * loc] + right

    acc_o = zero
    acc_i = zero
    for tap_z in range(3):
        for tap_y in range(3):
            base = tap_z * plane + tap_y * ROW
            pair = 3 * tap_z + tap_y
            sv = vs_ref[:, base : base + span]
            sc = cs_ref[:, base : base + span]
            acc_o = acc_o + shifted_sum(
                jnp.dot(wf_ref[pair], sv, preferred_element_type=jnp.float32)
            )
            acc_i = acc_i + shifted_sum(
                jnp.dot(wb_ref[pair], sc, preferred_element_type=jnp.float32)
            )
            w = lax.dot_general(
                sv, cstack, (((1,), (1,)), ((), ())), preferred_element_type=jnp.float32
            )
            for tap_x in range(3):
                wg_ref[3 * pair + tap_x] = w[:, tap_x * loc : (tap_x + 1) * loc]
    rows, cols = out_ref.shape[2], out_ref.shape[3]
    for z in range(planes):
        for acc, ref in ((acc_o, out_ref), (acc_i, ing_ref)):
            part = acc[:, z * plane : z * plane + width].reshape(loc, rows, cols)
            ref[:, z] = part.astype(ref.dtype)


def fused(own, far, near, low, high, far_low, far_high, halos, wf, wb, planes, width):
    both = own.shape[0]
    loc = both // 2
    cin = 4 * loc
    flat = (planes + 2) * (width + 2 * ROW)
    return pl.pallas_call(
        fused_kernel,
        out_shape=(
            jax.ShapeDtypeStruct((loc, planes, width // ROW, ROW), jnp.bfloat16),
            jax.ShapeDtypeStruct((loc, planes, width // ROW, ROW), jnp.bfloat16),
            jax.ShapeDtypeStruct((27, cin, loc), jnp.float32),
        ),
        scratch_shapes=[
            pltpu.VMEM((cin, flat), jnp.bfloat16),
            pltpu.VMEM((cin, flat), jnp.bfloat16),
        ],
    )(own, far, near, low, high, far_low, far_high, halos, wf, wb)


def by_group(array, order, size, dim):
    return jnp.concatenate(
        [lax.dynamic_slice_in_dim(array, group * size, size, dim) for group in order], axis=dim
    )


def body(volume, weight, cotangent):
    in_local, planes_local, grid_rows, grid_cols = volume.shape
    out_local = cotangent.shape[0]
    my_group = lax.axis_index(CH)
    slabs = lax.axis_size("gz")
    voxels = planes_local * slabs * grid_rows * grid_cols
    width = grid_rows * grid_cols
    both = jnp.concatenate([volume, cotangent], axis=0).reshape(in_local + out_local, -1)
    far, near = CH
    swap = [(0, 1), (1, 0)]
    up = [(i, i + 1) for i in range(slabs - 1)]
    down = [(j, i) for i, j in up]
    got_far = lax.ppermute(both, far, swap)
    low = lax.ppermute(both[:, -width:], "gz", up)
    high = lax.ppermute(both[:, :width], "gz", down)
    far_low = lax.ppermute(got_far[:, -width:], "gz", up)
    far_high = lax.ppermute(got_far[:, :width], "gz", down)
    got_near = lax.ppermute(jnp.stack([both, got_far]), near, swap)
    halos = lax.ppermute(jnp.stack([low, high, far_low, far_high]), near, swap)
    groups = 4
    order = [jnp.bitwise_xor(my_group, j) for j in range(groups)]
    cin = groups * in_local
    cout = groups * out_local
    weight_cols = lax.dynamic_slice_in_dim(weight, my_group * out_local, out_local, 2)
    weight_cols = by_group(weight_cols, order, in_local, 1)
    wf = jnp.transpose(weight_cols.reshape(3, 3, 3, cin, out_local), (0, 1, 2, 4, 3))
    wf = wf.reshape(9, 3 * out_local, cin)
    weight_rows = lax.dynamic_slice_in_dim(weight, my_group * in_local, in_local, 1)
    weight_rows = by_group(weight_rows, order, out_local, 2)
    wb = weight_rows[::-1].reshape(9, 3 * in_local, cout)
    out, ing, wg = fused(
        both, got_far, got_near, low, high, far_low, far_high, halos, wf, wb, planes_local, width
    )
    wg = by_group(wg, order, in_local, 1)
    shape = (out_local, planes_local, grid_rows, grid_cols)
    out = out.reshape(shape)
    ing = ing.reshape(shape)
    weight_grad = summed_on_arrival(wg.astype(jnp.bfloat16), "gz", 1) * jnp.float32(
        1.0 / math.sqrt(voxels)
    )
    return out, ing, weight_grad


def solution(mesh):
    split = Mesh(mesh.devices.reshape(mesh.shape["gz"], 2, 2), ("gz", "ch_0", "ch_1"))
    placed = (P(CH, "gz", None, None), P(), P(CH, "gz", None, None))
    return jax.shard_map(
        body,
        mesh=split,
        in_specs=placed,
        out_specs=(P(CH, "gz", None, None), P(CH, "gz", None, None), P(None, "gz", CH)),
        check_vma=False,
    )
```

```python
import math

import jax
import jax.numpy as jnp
from jax import lax
from jax.experimental import pallas as pl
from jax.experimental.pallas import tpu as pltpu
from jax.sharding import Mesh
from jax.sharding import PartitionSpec as P

CH = ("ch_0", "ch_1")
ROW = 128


def summed_on_arrival(shard, axis, dim):
    before, after = (shard.shape[:dim], shard.shape[dim + 1 :])
    devices = lax.axis_size(axis)
    blocks = jnp.moveaxis(shard.reshape(*before, devices, -1, *after), dim, 0)
    arrived = lax.all_to_all(blocks, axis, split_axis=0, concat_axis=0, tiled=True)
    return arrived.astype(jnp.float32).sum(axis=0)

def fused_kernel(
    own_ref, far_ref, near_ref, lo_ref, hi_ref, flo_ref, fhi_ref, hal_ref, wf_ref, wb_ref,
    out_ref, ing_ref, wg_ref, vs_ref, cs_ref,
):
    both = own_ref.shape[0]
    loc = both // 2
    planes = out_ref.shape[1]
    width = out_ref.shape[2] * out_ref.shape[3]
    plane = width + 2 * ROW
    span = (planes - 1) * plane + width
    blank = jnp.zeros((loc, ROW), jnp.bfloat16)
    pieces = (
        (lambda c: own_ref[c, :], lambda c: lo_ref[c, :], lambda c: hi_ref[c, :]),
        (lambda c: near_ref[0, c, :], lambda c: hal_ref[0, c, :], lambda c: hal_ref[1, c, :]),
        (lambda c: far_ref[c, :], lambda c: flo_ref[c, :], lambda c: fhi_ref[c, :]),
        (lambda c: near_ref[1, c, :], lambda c: hal_ref[2, c, :], lambda c: hal_ref[3, c, :]),
    )
    for k, (body_of, low_of, high_of) in enumerate(pieces):
        rows = slice(k * loc, (k + 1) * loc)
        for ref, low in ((vs_ref, 0), (cs_ref, loc)):
            chans = slice(low, low + loc)
            for zp in range(planes + 2):
                ref[rows, zp * plane : zp * plane + ROW] = blank
                ref[rows, zp * plane + ROW + width : (zp + 1) * plane] = blank
            ref[rows, ROW : ROW + width] = low_of(chans)
            for z in range(planes):
                at = (z + 1) * plane + ROW
                ref[rows, at : at + width] = body_of(chans)[:, z * width : (z + 1) * width]
            at = (planes + 1) * plane + ROW
            ref[rows, at : at + width] = high_of(chans)
    lane = lax.broadcasted_iota(jnp.int32, (loc, span), 1) % ROW
    first = lane == 0
    last = lane == ROW - 1
    zero = jnp.zeros((loc, span), jnp.float32)
    start = plane + ROW
    cm = cs_ref[0:loc, start : start + span].astype(jnp.float32)
    c_prev = jnp.where(last, zero, pltpu.roll(cm, span - 1, 1))
    c_next = jnp.where(first, zero, pltpu.roll(cm, 1, 1))
    cstack = jnp.concatenate([c_prev, cm, c_next], axis=0).astype(jnp.bfloat16)

    def shifted_sum(r):
        left = jnp.where(first, zero, pltpu.roll(r[0:loc], 1, 1))
        right = jnp.where(last, zero, pltpu.roll(r[2 * loc : 3 * loc], span - 1, 1))
        return left + r[loc : 2 * loc] + right

    acc_o = None
    acc_i = None
    for tap_z in range(3):
        for tap_y in range(3):
            base = tap_z * plane + tap_y * ROW
            pair = 3 * tap_z + tap_y
            sv = vs_ref[:, base : base + span]
            sc = cs_ref[:, base : base + span]
            r = jnp.dot(wf_ref[pair], sv, preferred_element_type=jnp.float32)
            acc_o = r if acc_o is None else acc_o + r
            r = jnp.dot(wb_ref[pair], sc, preferred_element_type=jnp.float32)
            acc_i = r if acc_i is None else acc_i + r
            w = lax.dot_general(
                sv, cstack, (((1,), (1,)), ((), ())), preferred_element_type=jnp.float32
            )
            for tap_x in range(3):
                wg_ref[3 * pair + tap_x] = w[:, tap_x * loc : (tap_x + 1) * loc]
    acc_o = shifted_sum(acc_o)
    acc_i = shifted_sum(acc_i)
    rows, cols = out_ref.shape[2], out_ref.shape[3]
    for z in range(planes):
        for acc, ref in ((acc_o, out_ref), (acc_i, ing_ref)):
            part = acc[:, z * plane : z * plane + width].reshape(loc, rows, cols)
            ref[:, z] = part.astype(ref.dtype)


def fused(own, far, near, low, high, far_low, far_high, halos, wf, wb, planes, width):
    both = own.shape[0]
    loc = both // 2
    cin = 4 * loc
    flat = (planes + 2) * (width + 2 * ROW)
    return pl.pallas_call(
        fused_kernel,
        out_shape=(
            jax.ShapeDtypeStruct((loc, planes, width // ROW, ROW), jnp.bfloat16),
            jax.ShapeDtypeStruct((loc, planes, width // ROW, ROW), jnp.bfloat16),
            jax.ShapeDtypeStruct((27, cin, loc), jnp.float32),
        ),
        scratch_shapes=[
            pltpu.VMEM((cin, flat), jnp.bfloat16),
            pltpu.VMEM((cin, flat), jnp.bfloat16),
        ],
    )(own, far, near, low, high, far_low, far_high, halos, wf, wb)


def by_group(array, order, size, dim):
    return jnp.concatenate(
        [lax.dynamic_slice_in_dim(array, group * size, size, dim) for group in order], axis=dim
    )


def body(volume, weight, cotangent):
    in_local, planes_local, grid_rows, grid_cols = volume.shape
    out_local = cotangent.shape[0]
    my_group = lax.axis_index(CH)
    slabs = lax.axis_size("gz")
    voxels = planes_local * slabs * grid_rows * grid_cols
    width = grid_rows * grid_cols
    both = jnp.concatenate([volume, cotangent], axis=0).reshape(in_local + out_local, -1)
    far, near = CH
    swap = [(0, 1), (1, 0)]
    up = [(i, i + 1) for i in range(slabs - 1)]
    down = [(j, i) for i, j in up]
    got_far = lax.ppermute(both, far, swap)
    low = lax.ppermute(both[:, -width:], "gz", up)
    high = lax.ppermute(both[:, :width], "gz", down)
    far_low = lax.ppermute(got_far[:, -width:], "gz", up)
    far_high = lax.ppermute(got_far[:, :width], "gz", down)
    got_near = lax.ppermute(jnp.stack([both, got_far]), near, swap)
    halos = lax.ppermute(jnp.stack([low, high, far_low, far_high]), near, swap)
    groups = 4
    order = [jnp.bitwise_xor(my_group, j) for j in range(groups)]
    cin = groups * in_local
    cout = groups * out_local
    weight_cols = lax.dynamic_slice_in_dim(weight, my_group * out_local, out_local, 2)
    weight_cols = by_group(weight_cols, order, in_local, 1)
    wf = jnp.transpose(weight_cols.reshape(3, 3, 3, cin, out_local), (0, 1, 2, 4, 3))
    wf = wf.reshape(9, 3 * out_local, cin)
    weight_rows = lax.dynamic_slice_in_dim(weight, my_group * in_local, in_local, 1)
    weight_rows = by_group(weight_rows, order, out_local, 2)
    wb = weight_rows[::-1].reshape(9, 3 * in_local, cout)
    out, ing, wg = fused(
        both, got_far, got_near, low, high, far_low, far_high, halos, wf, wb, planes_local, width
    )
    wg = by_group(wg, order, in_local, 1)
    shape = (out_local, planes_local, grid_rows, grid_cols)
    out = out.reshape(shape)
    ing = ing.reshape(shape)
    weight_grad = summed_on_arrival(wg.astype(jnp.bfloat16), "gz", 1) * jnp.float32(
        1.0 / math.sqrt(voxels)
    )
    return out, ing, weight_grad


def solution(mesh):
    split = Mesh(mesh.devices.reshape(mesh.shape["gz"], 2, 2), ("gz", "ch_0", "ch_1"))
    placed = (P(CH, "gz", None, None), P(), P(CH, "gz", None, None))
    return jax.shard_map(
        body,
        mesh=split,
        in_specs=placed,
        out_specs=(P(CH, "gz", None, None), P(CH, "gz", None, None), P(None, "gz", CH)),
        check_vma=False,
    )
```

```python
import math

import jax
import jax.numpy as jnp
from jax import lax
from jax.experimental import pallas as pl
from jax.experimental.pallas import tpu as pltpu
from jax.sharding import Mesh
from jax.sharding import PartitionSpec as P

CH = ("ch_0", "ch_1")
ROW = 128


def summed_on_arrival(shard, axis, dim):
    before, after = (shard.shape[:dim], shard.shape[dim + 1 :])
    devices = lax.axis_size(axis)
    blocks = jnp.moveaxis(shard.reshape(*before, devices, -1, *after), dim, 0)
    arrived = lax.all_to_all(blocks, axis, split_axis=0, concat_axis=0, tiled=True)
    return arrived.astype(jnp.float32).sum(axis=0)

def fused_kernel(
    own_ref, far_ref, near_ref, lo_ref, hi_ref, flo_ref, fhi_ref, hal_ref, wf_ref, wb_ref,
    out_ref, ing_ref, wg_ref, vs_ref, cs_ref, *, grads,
):
    both = own_ref.shape[0]
    loc = both // 2
    width = lo_ref.shape[1]
    planes = own_ref.shape[1] // width
    plane = width + 2 * ROW
    span = (planes - 1) * plane + width
    blank = jnp.zeros((loc, ROW), jnp.bfloat16)
    pieces = (
        (lambda c: own_ref[c, :], lambda c: lo_ref[c, :], lambda c: hi_ref[c, :]),
        (lambda c: near_ref[0, c, :], lambda c: hal_ref[0, c, :], lambda c: hal_ref[1, c, :]),
        (lambda c: far_ref[c, :], lambda c: flo_ref[c, :], lambda c: fhi_ref[c, :]),
        (lambda c: near_ref[1, c, :], lambda c: hal_ref[2, c, :], lambda c: hal_ref[3, c, :]),
    )
    for k, (body_of, low_of, high_of) in enumerate(pieces):
        rows = slice(k * loc, (k + 1) * loc)
        targets = ((vs_ref, 0), (cs_ref, loc)) if (not grads or k == 0) else ((vs_ref, 0),)
        for ref, low in targets:
            chans = slice(low, low + loc)
            for zp in range(planes + 2):
                ref[rows, zp * plane : zp * plane + ROW] = blank
                ref[rows, zp * plane + ROW + width : (zp + 1) * plane] = blank
            ref[rows, ROW : ROW + width] = low_of(chans)
            for z in range(planes):
                at = (z + 1) * plane + ROW
                ref[rows, at : at + width] = body_of(chans)[:, z * width : (z + 1) * width]
            at = (planes + 1) * plane + ROW
            ref[rows, at : at + width] = high_of(chans)
    lane = lax.broadcasted_iota(jnp.int32, (loc, span), 1) % ROW
    first = lane == 0
    last = lane == ROW - 1
    zero = jnp.zeros((loc, span), jnp.float32)
    if grads:
        start = plane + ROW
        cm = cs_ref[0:loc, start : start + span].astype(jnp.float32)
        c_prev = jnp.where(last, zero, pltpu.roll(cm, span - 1, 1))
        c_next = jnp.where(first, zero, pltpu.roll(cm, 1, 1))
        cstack = jnp.concatenate([c_prev, cm, c_next], axis=0).astype(jnp.bfloat16)

    def shifted_sum(r):
        left = jnp.where(first, zero, pltpu.roll(r[0:loc], 1, 1))
        right = jnp.where(last, zero, pltpu.roll(r[2 * loc : 3 * loc], span - 1, 1))
        return left + r[loc : 2 * loc] + right

    acc_o = None
    acc_i = None
    for tap_z in range(3):
        for tap_y in range(3):
            base = tap_z * plane + tap_y * ROW
            pair = 3 * tap_z + tap_y
            sv = vs_ref[:, base : base + span]
            if grads:
                w = lax.dot_general(
                    sv, cstack, (((1,), (1,)), ((), ())), preferred_element_type=jnp.float32
                )
                for tap_x in range(3):
                    wg_ref[3 * pair + tap_x] = w[:, tap_x * loc : (tap_x + 1) * loc]
                continue
            sc = cs_ref[:, base : base + span]
            r = jnp.dot(wf_ref[pair], sv, preferred_element_type=jnp.float32)
            acc_o = r if acc_o is None else acc_o + r
            r = jnp.dot(wb_ref[pair], sc, preferred_element_type=jnp.float32)
            acc_i = r if acc_i is None else acc_i + r
    if grads:
        return
    acc_o = shifted_sum(acc_o)
    acc_i = shifted_sum(acc_i)
    rows, cols = out_ref.shape[2], out_ref.shape[3]
    for z in range(planes):
        for acc, ref in ((acc_o, out_ref), (acc_i, ing_ref)):
            part = acc[:, z * plane : z * plane + width].reshape(loc, rows, cols)
            ref[:, z] = part.astype(ref.dtype)


def fused(pieces, wf, wb, planes, width, grads):
    both = pieces[0].shape[0]
    loc = both // 2
    cin = 4 * loc
    flat = (planes + 2) * (width + 2 * ROW)
    if grads:
        shapes = (jax.ShapeDtypeStruct((27, cin, loc), jnp.float32),)
    else:
        shapes = (
            jax.ShapeDtypeStruct((loc, planes, width // ROW, ROW), jnp.bfloat16),
            jax.ShapeDtypeStruct((loc, planes, width // ROW, ROW), jnp.bfloat16),
        )

    def kernel(*refs):
        ins = refs[:10]
        outs = refs[10:-2]
        if grads:
            outs = (None, None) + tuple(outs)
        else:
            outs = tuple(outs) + (None,)
        fused_kernel(*ins, *outs, *refs[-2:], grads=grads)

    return pl.pallas_call(
        kernel,
        out_shape=shapes,
        scratch_shapes=[
            pltpu.VMEM((cin, flat), jnp.bfloat16),
            pltpu.VMEM((cin, flat), jnp.bfloat16),
        ],
    )(*pieces, wf, wb)


def by_group(array, order, size, dim):
    return jnp.concatenate(
        [lax.dynamic_slice_in_dim(array, group * size, size, dim) for group in order], axis=dim
    )


def body(volume, weight, cotangent):
    in_local, planes_local, grid_rows, grid_cols = volume.shape
    out_local = cotangent.shape[0]
    my_group = lax.axis_index(CH)
    slabs = lax.axis_size("gz")
    voxels = planes_local * slabs * grid_rows * grid_cols
    width = grid_rows * grid_cols
    both = jnp.concatenate([volume, cotangent], axis=0).reshape(in_local + out_local, -1)
    far, near = CH
    swap = [(0, 1), (1, 0)]
    up = [(i, i + 1) for i in range(slabs - 1)]
    down = [(j, i) for i, j in up]
    got_far = lax.ppermute(both, far, swap)
    low = lax.ppermute(both[:, -width:], "gz", up)
    high = lax.ppermute(both[:, :width], "gz", down)
    far_low = lax.ppermute(got_far[:, -width:], "gz", up)
    far_high = lax.ppermute(got_far[:, :width], "gz", down)
    got_near = lax.ppermute(jnp.stack([both, got_far]), near, swap)
    halos = lax.ppermute(jnp.stack([low, high, far_low, far_high]), near, swap)
    groups = 4
    order = [jnp.bitwise_xor(my_group, j) for j in range(groups)]
    cin = groups * in_local
    cout = groups * out_local
    weight_cols = lax.dynamic_slice_in_dim(weight, my_group * out_local, out_local, 2)
    weight_cols = by_group(weight_cols, order, in_local, 1)
    wf = jnp.transpose(weight_cols.reshape(3, 3, 3, cin, out_local), (0, 1, 2, 4, 3))
    wf = wf.reshape(9, 3 * out_local, cin)
    weight_rows = lax.dynamic_slice_in_dim(weight, my_group * in_local, in_local, 1)
    weight_rows = by_group(weight_rows, order, out_local, 2)
    wb = weight_rows[::-1].reshape(9, 3 * in_local, cout)
    pieces = (both, got_far, got_near, low, high, far_low, far_high, halos)
    (wg,) = fused(pieces, wf, wb, planes_local, width, True)
    wg = by_group(wg, order, in_local, 1)
    out, ing = fused(pieces, wf, wb, planes_local, width, False)
    shape = (out_local, planes_local, grid_rows, grid_cols)
    out = out.reshape(shape)
    ing = ing.reshape(shape)
    weight_grad = summed_on_arrival(wg.astype(jnp.bfloat16), "gz", 1) * jnp.float32(
        1.0 / math.sqrt(voxels)
    )
    return out, ing, weight_grad


def solution(mesh):
    split = Mesh(mesh.devices.reshape(mesh.shape["gz"], 2, 2), ("gz", "ch_0", "ch_1"))
    placed = (P(CH, "gz", None, None), P(), P(CH, "gz", None, None))
    return jax.shard_map(
        body,
        mesh=split,
        in_specs=placed,
        out_specs=(P(CH, "gz", None, None), P(CH, "gz", None, None), P(None, "gz", CH)),
        check_vma=False,
    )
```

```python
import math

import jax
import jax.numpy as jnp
from jax import lax
from jax.experimental import pallas as pl
from jax.experimental.pallas import tpu as pltpu
from jax.sharding import Mesh
from jax.sharding import PartitionSpec as P

CH = ("ch_0", "ch_1")
ROW = 128


def summed_on_arrival(shard, axis, dim):
    before, after = (shard.shape[:dim], shard.shape[dim + 1 :])
    devices = lax.axis_size(axis)
    blocks = jnp.moveaxis(shard.reshape(*before, devices, -1, *after), dim, 0)
    arrived = lax.all_to_all(blocks, axis, split_axis=0, concat_axis=0, tiled=True)
    return arrived.astype(jnp.float32).sum(axis=0)

def fused_kernel(
    own_ref, far_ref, near_ref, lo_ref, hi_ref, flo_ref, fhi_ref, hal_ref, wf_ref, wb_ref,
    out_ref, ing_ref, wg_ref, vs_ref, cs_ref, *, grads,
):
    both = own_ref.shape[0]
    loc = both // 2
    width = lo_ref.shape[1]
    planes = own_ref.shape[1] // width
    plane = width + 2 * ROW
    span = (planes - 1) * plane + width
    blank = jnp.zeros((loc, ROW), jnp.bfloat16)
    pieces = (
        (lambda c: own_ref[c, :], lambda c: lo_ref[c, :], lambda c: hi_ref[c, :]),
        (lambda c: near_ref[0, c, :], lambda c: hal_ref[0, c, :], lambda c: hal_ref[1, c, :]),
        (lambda c: far_ref[c, :], lambda c: flo_ref[c, :], lambda c: fhi_ref[c, :]),
        (lambda c: near_ref[1, c, :], lambda c: hal_ref[2, c, :], lambda c: hal_ref[3, c, :]),
    )
    for k, (body_of, low_of, high_of) in enumerate(pieces):
        rows = slice(k * loc, (k + 1) * loc)
        targets = ((vs_ref, 0), (cs_ref, loc)) if (not grads or k == 0) else ((vs_ref, 0),)
        for ref, low in targets:
            chans = slice(low, low + loc)
            for zp in range(planes + 2):
                ref[rows, zp * plane : zp * plane + ROW] = blank
                ref[rows, zp * plane + ROW + width : (zp + 1) * plane] = blank
            ref[rows, ROW : ROW + width] = low_of(chans)
            for z in range(planes):
                at = (z + 1) * plane + ROW
                ref[rows, at : at + width] = body_of(chans)[:, z * width : (z + 1) * width]
            at = (planes + 1) * plane + ROW
            ref[rows, at : at + width] = high_of(chans)
    lane = lax.broadcasted_iota(jnp.int32, (loc, span), 1) % ROW
    first = lane == 0
    last = lane == ROW - 1
    zero = jnp.zeros((loc, span), jnp.float32)
    if grads:
        start = plane + ROW
        cm = cs_ref[0:loc, start : start + span].astype(jnp.float32)
        c_prev = jnp.where(last, zero, pltpu.roll(cm, span - 1, 1))
        c_next = jnp.where(first, zero, pltpu.roll(cm, 1, 1))
        cstack = jnp.concatenate([c_prev, cm, c_next], axis=0).astype(jnp.bfloat16)

    def shifted_sum(r):
        left = jnp.where(first, zero, pltpu.roll(r[0:loc], 1, 1))
        right = jnp.where(last, zero, pltpu.roll(r[2 * loc : 3 * loc], span - 1, 1))
        return left + r[loc : 2 * loc] + right

    acc_o = None
    acc_i = None
    for tap_z in range(3):
        for tap_y in range(3):
            base = tap_z * plane + tap_y * ROW
            pair = 3 * tap_z + tap_y
            sv = vs_ref[:, base : base + span]
            if grads:
                w = lax.dot_general(
                    sv, cstack, (((1,), (1,)), ((), ())), preferred_element_type=jnp.float32
                )
                for tap_x in range(3):
                    wg_ref[3 * pair + tap_x] = w[:, tap_x * loc : (tap_x + 1) * loc]
                continue
            sc = cs_ref[:, base : base + span]
            r = jnp.dot(wf_ref[pair], sv, preferred_element_type=jnp.float32)
            acc_o = r if acc_o is None else acc_o + r
            r = jnp.dot(wb_ref[pair], sc, preferred_element_type=jnp.float32)
            acc_i = r if acc_i is None else acc_i + r
    if grads:
        return
    acc_o = shifted_sum(acc_o)
    acc_i = shifted_sum(acc_i)
    rows, cols = out_ref.shape[2], out_ref.shape[3]
    for z in range(planes):
        for acc, ref in ((acc_o, out_ref), (acc_i, ing_ref)):
            part = acc[:, z * plane : z * plane + width].reshape(loc, rows, cols)
            ref[:, z] = part.astype(ref.dtype)


def fused(pieces, wf, wb, planes, width, grads):
    both = pieces[0].shape[0]
    loc = both // 2
    cin = 4 * loc
    flat = (planes + 2) * (width + 2 * ROW)
    if grads:
        shapes = (jax.ShapeDtypeStruct((27, cin, loc), jnp.float32),)
    else:
        shapes = (
            jax.ShapeDtypeStruct((loc, planes, width // ROW, ROW), jnp.bfloat16),
            jax.ShapeDtypeStruct((loc, planes, width // ROW, ROW), jnp.bfloat16),
        )

    count = len(pieces) if grads else len(pieces) + 2

    def kernel(*refs):
        ins = refs[:count]
        outs = refs[count:-2]
        if grads:
            ins = tuple(ins) + (None, None)
            outs = (None, None) + tuple(outs)
        else:
            outs = tuple(outs) + (None,)
        fused_kernel(*ins, *outs, *refs[-2:], grads=grads)

    return pl.pallas_call(
        kernel,
        out_shape=shapes,
        scratch_shapes=[
            pltpu.VMEM((cin, flat), jnp.bfloat16),
            pltpu.VMEM((cin, flat), jnp.bfloat16),
        ],
    )(*(pieces if grads else pieces + (wf, wb)))


def by_group(array, order, size, dim):
    return jnp.concatenate(
        [lax.dynamic_slice_in_dim(array, group * size, size, dim) for group in order], axis=dim
    )


def body(volume, weight, cotangent):
    in_local, planes_local, grid_rows, grid_cols = volume.shape
    out_local = cotangent.shape[0]
    my_group = lax.axis_index(CH)
    slabs = lax.axis_size("gz")
    voxels = planes_local * slabs * grid_rows * grid_cols
    width = grid_rows * grid_cols
    both = jnp.concatenate([volume, cotangent], axis=0).reshape(in_local + out_local, -1)
    far, near = CH
    swap = [(0, 1), (1, 0)]
    up = [(i, i + 1) for i in range(slabs - 1)]
    down = [(j, i) for i, j in up]
    got_far = lax.ppermute(both, far, swap)
    low = lax.ppermute(both[:, -width:], "gz", up)
    high = lax.ppermute(both[:, :width], "gz", down)
    far_low = lax.ppermute(got_far[:, -width:], "gz", up)
    far_high = lax.ppermute(got_far[:, :width], "gz", down)
    got_near = lax.ppermute(jnp.stack([both, got_far]), near, swap)
    halos = lax.ppermute(jnp.stack([low, high, far_low, far_high]), near, swap)
    groups = 4
    order = [jnp.bitwise_xor(my_group, j) for j in range(groups)]
    cin = groups * in_local
    cout = groups * out_local
    weight_cols = lax.dynamic_slice_in_dim(weight, my_group * out_local, out_local, 2)
    weight_cols = by_group(weight_cols, order, in_local, 1)
    wf = jnp.transpose(weight_cols.reshape(3, 3, 3, cin, out_local), (0, 1, 2, 4, 3))
    wf = wf.reshape(9, 3 * out_local, cin)
    weight_rows = lax.dynamic_slice_in_dim(weight, my_group * in_local, in_local, 1)
    weight_rows = by_group(weight_rows, order, out_local, 2)
    wb = weight_rows[::-1].reshape(9, 3 * in_local, cout)
    pieces = (both, got_far, got_near, low, high, far_low, far_high, halos)
    (wg,) = fused(pieces, wf, wb, planes_local, width, True)
    wg = by_group(wg, order, in_local, 1)
    out, ing = fused(pieces, wf, wb, planes_local, width, False)
    shape = (out_local, planes_local, grid_rows, grid_cols)
    out = out.reshape(shape)
    ing = ing.reshape(shape)
    weight_grad = summed_on_arrival(wg.astype(jnp.bfloat16), "gz", 1) * jnp.float32(
        1.0 / math.sqrt(voxels)
    )
    return out, ing, weight_grad


def solution(mesh):
    split = Mesh(mesh.devices.reshape(mesh.shape["gz"], 2, 2), ("gz", "ch_0", "ch_1"))
    placed = (P(CH, "gz", None, None), P(), P(CH, "gz", None, None))
    return jax.shard_map(
        body,
        mesh=split,
        in_specs=placed,
        out_specs=(P(CH, "gz", None, None), P(CH, "gz", None, None), P(None, "gz", CH)),
        check_vma=False,
    )
```

```python
import math

import jax
import jax.numpy as jnp
from jax import lax
from jax.experimental import pallas as pl
from jax.experimental.pallas import tpu as pltpu
from jax.sharding import Mesh
from jax.sharding import PartitionSpec as P

CH = ("ch_0", "ch_1")
ROW = 128


def summed_on_arrival(shard, axis, dim):
    before, after = (shard.shape[:dim], shard.shape[dim + 1 :])
    devices = lax.axis_size(axis)
    blocks = jnp.moveaxis(shard.reshape(*before, devices, -1, *after), dim, 0)
    arrived = lax.all_to_all(blocks, axis, split_axis=0, concat_axis=0, tiled=True)
    return arrived.astype(jnp.float32).sum(axis=0)

def fused_kernel(
    own_ref, far_ref, near_ref, lo_ref, hi_ref, flo_ref, fhi_ref, hal_ref, wf_ref, wb_ref,
    out_ref, ing_ref, wg_ref, vs_ref, cs_ref, *, grads,
):
    both = own_ref.shape[0]
    loc = both // 2
    width = lo_ref.shape[1]
    planes = own_ref.shape[1] // width
    plane = width + 2 * ROW
    span = (planes - 1) * plane + width
    blank = jnp.zeros((loc, ROW), jnp.bfloat16)
    pieces = (
        (lambda c: own_ref[c, :], lambda c: lo_ref[c, :], lambda c: hi_ref[c, :]),
        (lambda c: near_ref[0, c, :], lambda c: hal_ref[0, c, :], lambda c: hal_ref[1, c, :]),
        (lambda c: far_ref[c, :], lambda c: flo_ref[c, :], lambda c: fhi_ref[c, :]),
        (lambda c: near_ref[1, c, :], lambda c: hal_ref[2, c, :], lambda c: hal_ref[3, c, :]),
    )
    for k, (body_of, low_of, high_of) in enumerate(pieces):
        rows = slice(k * loc, (k + 1) * loc)
        targets = ((vs_ref, 0), (cs_ref, loc)) if (not grads or k == 0) else ((vs_ref, 0),)
        for ref, low in targets:
            chans = slice(low, low + loc)
            for zp in range(planes + 2):
                ref[rows, zp * plane : zp * plane + ROW] = blank
                ref[rows, zp * plane + ROW + width : (zp + 1) * plane] = blank
            ref[rows, ROW : ROW + width] = low_of(chans)
            for z in range(planes):
                at = (z + 1) * plane + ROW
                ref[rows, at : at + width] = body_of(chans)[:, z * width : (z + 1) * width]
            at = (planes + 1) * plane + ROW
            ref[rows, at : at + width] = high_of(chans)
    lane = lax.broadcasted_iota(jnp.int32, (loc, span), 1) % ROW
    first = lane == 0
    last = lane == ROW - 1
    zero = jnp.zeros((loc, span), jnp.float32)
    if grads:
        start = plane + ROW
        cm = cs_ref[0:loc, start : start + span].astype(jnp.float32)
        c_prev = jnp.where(last, zero, pltpu.roll(cm, span - 1, 1))
        c_next = jnp.where(first, zero, pltpu.roll(cm, 1, 1))
        cstack = jnp.concatenate([c_prev, cm, c_next], axis=0).astype(jnp.bfloat16)

    def shifted_sum(r):
        left = jnp.where(first, zero, pltpu.roll(r[0:loc], 1, 1))
        right = jnp.where(last, zero, pltpu.roll(r[2 * loc : 3 * loc], span - 1, 1))
        return left + r[loc : 2 * loc] + right

    acc_o = None
    acc_i = None
    for tap_z in range(3):
        for tap_y in range(3):
            base = tap_z * plane + tap_y * ROW
            pair = 3 * tap_z + tap_y
            sv = vs_ref[:, base : base + span]
            if grads:
                w = lax.dot_general(
                    sv, cstack, (((1,), (1,)), ((), ())), preferred_element_type=jnp.float32
                )
                for tap_x in range(3):
                    wg_ref[3 * pair + tap_x] = w[:, tap_x * loc : (tap_x + 1) * loc]
                continue
            sc = cs_ref[:, base : base + span]
            r = jnp.dot(wf_ref[pair], sv, preferred_element_type=jnp.float32)
            acc_o = r if acc_o is None else acc_o + r
            r = jnp.dot(wb_ref[pair], sc, preferred_element_type=jnp.float32)
            acc_i = r if acc_i is None else acc_i + r
    if grads:
        return
    acc_o = shifted_sum(acc_o)
    acc_i = shifted_sum(acc_i)
    rows, cols = out_ref.shape[2], out_ref.shape[3]
    for z in range(planes):
        for acc, ref in ((acc_o, out_ref), (acc_i, ing_ref)):
            part = acc[:, z * plane : z * plane + width].reshape(loc, rows, cols)
            ref[:, z] = part.astype(ref.dtype)


def fused(pieces, wf, wb, planes, width, grads):
    both = pieces[0].shape[0]
    loc = both // 2
    cin = 4 * loc
    flat = (planes + 2) * (width + 2 * ROW)
    if grads:
        shapes = (jax.ShapeDtypeStruct((27, cin, loc), jnp.float32),)
    else:
        shapes = (
            jax.ShapeDtypeStruct((loc, planes, width // ROW, ROW), jnp.bfloat16),
            jax.ShapeDtypeStruct((loc, planes, width // ROW, ROW), jnp.bfloat16),
        )

    count = len(pieces) if grads else len(pieces) + 2

    def kernel(*refs):
        ins = refs[:count]
        outs = refs[count:-2]
        if grads:
            ins = tuple(ins) + (None, None)
            outs = (None, None) + tuple(outs)
        else:
            outs = tuple(outs) + (None,)
        fused_kernel(*ins, *outs, *refs[-2:], grads=grads)

    return pl.pallas_call(
        kernel,
        out_shape=shapes,
        scratch_shapes=[
            pltpu.VMEM((cin, flat), jnp.bfloat16),
            pltpu.VMEM((cin, flat), jnp.bfloat16),
        ],
    )(*(pieces if grads else pieces + (wf, wb)))


def by_group(array, order, size, dim):
    return jnp.concatenate(
        [lax.dynamic_slice_in_dim(array, group * size, size, dim) for group in order], axis=dim
    )


def body(volume, weight, cotangent):
    in_local, planes_local, grid_rows, grid_cols = volume.shape
    out_local = cotangent.shape[0]
    my_group = lax.axis_index(CH)
    slabs = lax.axis_size("gz")
    voxels = planes_local * slabs * grid_rows * grid_cols
    width = grid_rows * grid_cols
    both = jnp.concatenate([volume, cotangent], axis=0).reshape(in_local + out_local, -1)
    far, near = CH
    swap = [(0, 1), (1, 0)]
    up = [(i, i + 1) for i in range(slabs - 1)]
    down = [(j, i) for i, j in up]
    got_far = lax.ppermute(both, far, swap)
    low = lax.ppermute(both[:, -width:], "gz", up)
    high = lax.ppermute(both[:, :width], "gz", down)
    groups = 4
    order = [jnp.bitwise_xor(my_group, j) for j in range(groups)]
    cin = groups * in_local
    cout = groups * out_local
    weight_cols = lax.dynamic_slice_in_dim(weight, my_group * out_local, out_local, 2)
    weight_cols = by_group(weight_cols, order, in_local, 1)
    wf = jnp.transpose(weight_cols.reshape(3, 3, 3, cin, out_local), (0, 1, 2, 4, 3))
    wf = wf.reshape(9, 3 * out_local, cin)
    weight_rows = lax.dynamic_slice_in_dim(weight, my_group * in_local, in_local, 1)
    weight_rows = by_group(weight_rows, order, out_local, 2)
    wb = weight_rows[::-1].reshape(9, 3 * in_local, cout)
    got_far, wf, wb = lax.optimization_barrier((got_far, wf, wb))
    far_low = lax.ppermute(got_far[:, -width:], "gz", up)
    far_high = lax.ppermute(got_far[:, :width], "gz", down)
    got_near = lax.ppermute(jnp.stack([both, got_far]), near, swap)
    halos = lax.ppermute(jnp.stack([low, high, far_low, far_high]), near, swap)
    pieces = (both, got_far, got_near, low, high, far_low, far_high, halos)
    (wg,) = fused(pieces, wf, wb, planes_local, width, True)
    wg = by_group(wg, order, in_local, 1)
    out, ing = fused(pieces, wf, wb, planes_local, width, False)
    shape = (out_local, planes_local, grid_rows, grid_cols)
    out = out.reshape(shape)
    ing = ing.reshape(shape)
    weight_grad = summed_on_arrival(wg.astype(jnp.bfloat16), "gz", 1) * jnp.float32(
        1.0 / math.sqrt(voxels)
    )
    return out, ing, weight_grad


def solution(mesh):
    split = Mesh(mesh.devices.reshape(mesh.shape["gz"], 2, 2), ("gz", "ch_0", "ch_1"))
    placed = (P(CH, "gz", None, None), P(), P(CH, "gz", None, None))
    return jax.shard_map(
        body,
        mesh=split,
        in_specs=placed,
        out_specs=(P(CH, "gz", None, None), P(CH, "gz", None, None), P(None, "gz", CH)),
        check_vma=False,
    )
```

```python
import math

import jax
import jax.numpy as jnp
from jax import lax
from jax.experimental import pallas as pl
from jax.experimental.pallas import tpu as pltpu
from jax.sharding import Mesh
from jax.sharding import PartitionSpec as P

CH = ("ch_0", "ch_1")
ROW = 128


def summed_on_arrival(shard, axis, dim):
    before, after = (shard.shape[:dim], shard.shape[dim + 1 :])
    devices = lax.axis_size(axis)
    blocks = jnp.moveaxis(shard.reshape(*before, devices, -1, *after), dim, 0)
    arrived = lax.all_to_all(blocks, axis, split_axis=0, concat_axis=0, tiled=True)
    return arrived.astype(jnp.float32).sum(axis=0)

def fused_kernel(
    own_ref, far_ref, near_ref, lo_ref, hi_ref, flo_ref, fhi_ref, ohal_ref, fhal_ref, wf_ref, wb_ref,
    out_ref, ing_ref, wg_ref, vs_ref, cs_ref,
):
    both = own_ref.shape[0]
    loc = both // 2
    planes = out_ref.shape[1]
    width = out_ref.shape[2] * out_ref.shape[3]
    plane = width + 2 * ROW
    span = (planes - 1) * plane + width
    blank = jnp.zeros((loc, ROW), jnp.bfloat16)
    pieces = (
        (lambda c: own_ref[c, :], lambda c: lo_ref[c, :], lambda c: hi_ref[c, :]),
        (lambda c: near_ref[0, c, :], lambda c: ohal_ref[0, c, :], lambda c: ohal_ref[1, c, :]),
        (lambda c: far_ref[c, :], lambda c: flo_ref[c, :], lambda c: fhi_ref[c, :]),
        (lambda c: near_ref[1, c, :], lambda c: fhal_ref[0, c, :], lambda c: fhal_ref[1, c, :]),
    )
    for k, (body_of, low_of, high_of) in enumerate(pieces):
        rows = slice(k * loc, (k + 1) * loc)
        for ref, low in ((vs_ref, 0), (cs_ref, loc)):
            chans = slice(low, low + loc)
            for zp in range(planes + 2):
                ref[rows, zp * plane : zp * plane + ROW] = blank
                ref[rows, zp * plane + ROW + width : (zp + 1) * plane] = blank
            ref[rows, ROW : ROW + width] = low_of(chans)
            for z in range(planes):
                at = (z + 1) * plane + ROW
                ref[rows, at : at + width] = body_of(chans)[:, z * width : (z + 1) * width]
            at = (planes + 1) * plane + ROW
            ref[rows, at : at + width] = high_of(chans)
    lane = lax.broadcasted_iota(jnp.int32, (loc, span), 1) % ROW
    first = lane == 0
    last = lane == ROW - 1
    zero = jnp.zeros((loc, span), jnp.float32)
    start = plane + ROW
    cm = cs_ref[0:loc, start : start + span].astype(jnp.float32)
    c_prev = jnp.where(last, zero, pltpu.roll(cm, span - 1, 1))
    c_next = jnp.where(first, zero, pltpu.roll(cm, 1, 1))
    cstack = jnp.concatenate([c_prev, cm, c_next], axis=0).astype(jnp.bfloat16)

    def shifted_sum(r):
        left = jnp.where(first, zero, pltpu.roll(r[0:loc], 1, 1))
        right = jnp.where(last, zero, pltpu.roll(r[2 * loc : 3 * loc], span - 1, 1))
        return left + r[loc : 2 * loc] + right

    acc_o = None
    acc_i = None
    for tap_z in range(3):
        for tap_y in range(3):
            base = tap_z * plane + tap_y * ROW
            pair = 3 * tap_z + tap_y
            sv = vs_ref[:, base : base + span]
            sc = cs_ref[:, base : base + span]
            r = jnp.dot(wf_ref[pair], sv, preferred_element_type=jnp.float32)
            acc_o = r if acc_o is None else acc_o + r
            r = jnp.dot(wb_ref[pair], sc, preferred_element_type=jnp.float32)
            acc_i = r if acc_i is None else acc_i + r
            w = lax.dot_general(
                sv, cstack, (((1,), (1,)), ((), ())), preferred_element_type=jnp.float32
            )
            for tap_x in range(3):
                wg_ref[3 * pair + tap_x] = w[:, tap_x * loc : (tap_x + 1) * loc]
    acc_o = shifted_sum(acc_o)
    acc_i = shifted_sum(acc_i)
    rows, cols = out_ref.shape[2], out_ref.shape[3]
    for z in range(planes):
        for acc, ref in ((acc_o, out_ref), (acc_i, ing_ref)):
            part = acc[:, z * plane : z * plane + width].reshape(loc, rows, cols)
            ref[:, z] = part.astype(ref.dtype)


def fused(own, far, near, low, high, far_low, far_high, own_halos, far_halos, wf, wb, planes, width):
    both = own.shape[0]
    loc = both // 2
    cin = 4 * loc
    flat = (planes + 2) * (width + 2 * ROW)
    return pl.pallas_call(
        fused_kernel,
        out_shape=(
            jax.ShapeDtypeStruct((loc, planes, width // ROW, ROW), jnp.bfloat16),
            jax.ShapeDtypeStruct((loc, planes, width // ROW, ROW), jnp.bfloat16),
            jax.ShapeDtypeStruct((27, cin, loc), jnp.float32),
        ),
        scratch_shapes=[
            pltpu.VMEM((cin, flat), jnp.bfloat16),
            pltpu.VMEM((cin, flat), jnp.bfloat16),
        ],
    )(own, far, near, low, high, far_low, far_high, own_halos, far_halos, wf, wb)


def by_group(array, order, size, dim):
    return jnp.concatenate(
        [lax.dynamic_slice_in_dim(array, group * size, size, dim) for group in order], axis=dim
    )


def body(volume, weight, cotangent):
    in_local, planes_local, grid_rows, grid_cols = volume.shape
    out_local = cotangent.shape[0]
    my_group = lax.axis_index(CH)
    slabs = lax.axis_size("gz")
    voxels = planes_local * slabs * grid_rows * grid_cols
    width = grid_rows * grid_cols
    both = jnp.concatenate([volume, cotangent], axis=0).reshape(in_local + out_local, -1)
    far, near = CH
    swap = [(0, 1), (1, 0)]
    up = [(i, i + 1) for i in range(slabs - 1)]
    down = [(j, i) for i, j in up]
    got_far = lax.ppermute(both, far, swap)
    low = lax.ppermute(both[:, -width:], "gz", up)
    high = lax.ppermute(both[:, :width], "gz", down)
    far_low = lax.ppermute(got_far[:, -width:], "gz", up)
    far_high = lax.ppermute(got_far[:, :width], "gz", down)
    got_near = lax.ppermute(jnp.stack([both, got_far]), near, swap)
    own_halos = lax.ppermute(jnp.stack([low, high]), near, swap)
    far_halos = lax.ppermute(jnp.stack([far_low, far_high]), near, swap)
    groups = 4
    order = [jnp.bitwise_xor(my_group, j) for j in range(groups)]
    cin = groups * in_local
    cout = groups * out_local
    weight_cols = lax.dynamic_slice_in_dim(weight, my_group * out_local, out_local, 2)
    weight_cols = by_group(weight_cols, order, in_local, 1)
    wf = jnp.transpose(weight_cols.reshape(3, 3, 3, cin, out_local), (0, 1, 2, 4, 3))
    wf = wf.reshape(9, 3 * out_local, cin)
    weight_rows = lax.dynamic_slice_in_dim(weight, my_group * in_local, in_local, 1)
    weight_rows = by_group(weight_rows, order, out_local, 2)
    wb = weight_rows[::-1].reshape(9, 3 * in_local, cout)
    out, ing, wg = fused(
        both, got_far, got_near, low, high, far_low, far_high, own_halos, far_halos, wf, wb,
        planes_local, width,
    )
    wg = by_group(wg, order, in_local, 1)
    shape = (out_local, planes_local, grid_rows, grid_cols)
    out = out.reshape(shape)
    ing = ing.reshape(shape)
    weight_grad = summed_on_arrival(wg.astype(jnp.bfloat16), "gz", 1) * jnp.float32(
        1.0 / math.sqrt(voxels)
    )
    return out, ing, weight_grad


def solution(mesh):
    split = Mesh(mesh.devices.reshape(mesh.shape["gz"], 2, 2), ("gz", "ch_0", "ch_1"))
    placed = (P(CH, "gz", None, None), P(), P(CH, "gz", None, None))
    return jax.shard_map(
        body,
        mesh=split,
        in_specs=placed,
        out_specs=(P(CH, "gz", None, None), P(CH, "gz", None, None), P(None, "gz", CH)),
        check_vma=False,
    )
```

```python
import math

import jax
import jax.numpy as jnp
from jax import lax
from jax.experimental import pallas as pl
from jax.experimental.pallas import tpu as pltpu
from jax.sharding import Mesh
from jax.sharding import PartitionSpec as P

CH = ("ch_0", "ch_1")
ROW = 128


def summed_on_arrival(shard, axis, dim):
    before, after = (shard.shape[:dim], shard.shape[dim + 1 :])
    devices = lax.axis_size(axis)
    blocks = jnp.moveaxis(shard.reshape(*before, devices, -1, *after), dim, 0)
    arrived = lax.all_to_all(blocks, axis, split_axis=0, concat_axis=0, tiled=True)
    return arrived.astype(jnp.float32).sum(axis=0)

def fused_kernel(
    own_ref, far_ref, near_ref, lo_ref, hi_ref, flo_ref, fhi_ref, hal_ref, wf_ref, wb_ref,
    out_ref, ing_ref, wg_ref, vs_ref, cs_ref,
):
    both = own_ref.shape[0]
    loc = both // 2
    planes = out_ref.shape[1]
    width = out_ref.shape[2] * out_ref.shape[3]
    plane = width + 2 * ROW
    span = (planes - 1) * plane + width
    blank = jnp.zeros((loc, ROW), jnp.bfloat16)
    pieces = (
        (lambda c: own_ref[c, :], lambda c: lo_ref[c, :], lambda c: hi_ref[c, :]),
        (lambda c: near_ref[0, c, :], lambda c: hal_ref[0, c, :], lambda c: hal_ref[1, c, :]),
        (lambda c: far_ref[c, :], lambda c: flo_ref[c, :], lambda c: fhi_ref[c, :]),
        (lambda c: near_ref[1, c, :], lambda c: hal_ref[2, c, :], lambda c: hal_ref[3, c, :]),
    )
    for k, (body_of, low_of, high_of) in enumerate(pieces):
        rows = slice(k * loc, (k + 1) * loc)
        for ref, low in ((vs_ref, 0), (cs_ref, loc)):
            chans = slice(low, low + loc)
            for zp in range(planes + 2):
                ref[rows, zp * plane : zp * plane + ROW] = blank
                ref[rows, zp * plane + ROW + width : (zp + 1) * plane] = blank
            ref[rows, ROW : ROW + width] = low_of(chans)
            for z in range(planes):
                at = (z + 1) * plane + ROW
                ref[rows, at : at + width] = body_of(chans)[:, z * width : (z + 1) * width]
            at = (planes + 1) * plane + ROW
            ref[rows, at : at + width] = high_of(chans)
    lane = lax.broadcasted_iota(jnp.int32, (loc, span), 1) % ROW
    first = lane == 0
    last = lane == ROW - 1
    zero = jnp.zeros((loc, span), jnp.float32)
    start = plane + ROW
    cm = cs_ref[0:loc, start : start + span].astype(jnp.float32)
    c_prev = jnp.where(last, zero, pltpu.roll(cm, span - 1, 1))
    c_next = jnp.where(first, zero, pltpu.roll(cm, 1, 1))
    cstack = jnp.concatenate([c_prev, cm, c_next], axis=0).astype(jnp.bfloat16)

    def shifted_sum(r):
        left = jnp.where(first, zero, pltpu.roll(r[0:loc], 1, 1))
        right = jnp.where(last, zero, pltpu.roll(r[2 * loc : 3 * loc], span - 1, 1))
        return left + r[loc : 2 * loc] + right

    acc_o = None
    acc_i = None
    for tap_z in range(3):
        for tap_y in range(3):
            base = tap_z * plane + tap_y * ROW
            pair = 3 * tap_z + tap_y
            sv = vs_ref[:, base : base + span]
            sc = cs_ref[:, base : base + span]
            r = jnp.dot(wf_ref[pair], sv, preferred_element_type=jnp.float32)
            acc_o = r if acc_o is None else acc_o + r
            r = jnp.dot(wb_ref[pair], sc, preferred_element_type=jnp.float32)
            acc_i = r if acc_i is None else acc_i + r
            w = lax.dot_general(
                sv, cstack, (((1,), (1,)), ((), ())), preferred_element_type=jnp.float32
            )
            for tap_x in range(3):
                wg_ref[3 * pair + tap_x] = w[:, tap_x * loc : (tap_x + 1) * loc]
    acc_o = shifted_sum(acc_o)
    acc_i = shifted_sum(acc_i)
    rows, cols = out_ref.shape[2], out_ref.shape[3]
    for z in range(planes):
        for acc, ref in ((acc_o, out_ref), (acc_i, ing_ref)):
            part = acc[:, z * plane : z * plane + width].reshape(loc, rows, cols)
            ref[:, z] = part.astype(ref.dtype)


def fused(own, far, near, low, high, far_low, far_high, halos, wf, wb, planes, width):
    both = own.shape[0]
    loc = both // 2
    cin = 4 * loc
    flat = (planes + 2) * (width + 2 * ROW)
    return pl.pallas_call(
        fused_kernel,
        out_shape=(
            jax.ShapeDtypeStruct((loc, planes, width // ROW, ROW), jnp.bfloat16),
            jax.ShapeDtypeStruct((loc, planes, width // ROW, ROW), jnp.bfloat16),
            jax.ShapeDtypeStruct((27, cin, loc), jnp.float32),
        ),
        scratch_shapes=[
            pltpu.VMEM((cin, flat), jnp.bfloat16),
            pltpu.VMEM((cin, flat), jnp.bfloat16),
        ],
    )(own, far, near, low, high, far_low, far_high, halos, wf, wb)


def by_group(array, order, size, dim):
    return jnp.concatenate(
        [lax.dynamic_slice_in_dim(array, group * size, size, dim) for group in order], axis=dim
    )


def body(volume, weight, cotangent):
    in_local, planes_local, grid_rows, grid_cols = volume.shape
    out_local = cotangent.shape[0]
    my_group = lax.axis_index(CH)
    slabs = lax.axis_size("gz")
    voxels = planes_local * slabs * grid_rows * grid_cols
    width = grid_rows * grid_cols
    both = jnp.concatenate([volume, cotangent], axis=0).reshape(in_local + out_local, -1)
    far, near = CH
    swap = [(0, 1), (1, 0)]
    up = [(i, i + 1) for i in range(slabs - 1)]
    down = [(j, i) for i, j in up]
    far_vol, far_cot = lax.ppermute((volume, cotangent), far, swap)
    got_far = jnp.concatenate([far_vol, far_cot], axis=0).reshape(both.shape)
    low = lax.ppermute(both[:, -width:], "gz", up)
    high = lax.ppermute(both[:, :width], "gz", down)
    far_low = lax.ppermute(got_far[:, -width:], "gz", up)
    far_high = lax.ppermute(got_far[:, :width], "gz", down)
    got_near = lax.ppermute(jnp.stack([both, got_far]), near, swap)
    halos = lax.ppermute(jnp.stack([low, high, far_low, far_high]), near, swap)
    groups = 4
    order = [jnp.bitwise_xor(my_group, j) for j in range(groups)]
    cin = groups * in_local
    cout = groups * out_local
    weight_cols = lax.dynamic_slice_in_dim(weight, my_group * out_local, out_local, 2)
    weight_cols = by_group(weight_cols, order, in_local, 1)
    wf = jnp.transpose(weight_cols.reshape(3, 3, 3, cin, out_local), (0, 1, 2, 4, 3))
    wf = wf.reshape(9, 3 * out_local, cin)
    weight_rows = lax.dynamic_slice_in_dim(weight, my_group * in_local, in_local, 1)
    weight_rows = by_group(weight_rows, order, out_local, 2)
    wb = weight_rows[::-1].reshape(9, 3 * in_local, cout)
    out, ing, wg = fused(
        both, got_far, got_near, low, high, far_low, far_high, halos, wf, wb, planes_local, width
    )
    wg = by_group(wg, order, in_local, 1)
    shape = (out_local, planes_local, grid_rows, grid_cols)
    out = out.reshape(shape)
    ing = ing.reshape(shape)
    weight_grad = summed_on_arrival(wg.astype(jnp.bfloat16), "gz", 1) * jnp.float32(
        1.0 / math.sqrt(voxels)
    )
    return out, ing, weight_grad


def solution(mesh):
    split = Mesh(mesh.devices.reshape(mesh.shape["gz"], 2, 2), ("gz", "ch_0", "ch_1"))
    placed = (P(CH, "gz", None, None), P(), P(CH, "gz", None, None))
    return jax.shard_map(
        body,
        mesh=split,
        in_specs=placed,
        out_specs=(P(CH, "gz", None, None), P(CH, "gz", None, None), P(None, "gz", CH)),
        check_vma=False,
    )
```

```python
import math

import jax
import jax.numpy as jnp
from jax import lax
from jax.experimental import pallas as pl
from jax.experimental.pallas import tpu as pltpu
from jax.sharding import Mesh
from jax.sharding import PartitionSpec as P

CH = ("ch_0", "ch_1")
ROW = 128


def summed_on_arrival(shard, axis, dim):
    before, after = (shard.shape[:dim], shard.shape[dim + 1 :])
    devices = lax.axis_size(axis)
    blocks = jnp.moveaxis(shard.reshape(*before, devices, -1, *after), dim, 0)
    arrived = lax.all_to_all(blocks, axis, split_axis=0, concat_axis=0, tiled=True)
    return arrived.astype(jnp.float32).sum(axis=0)

def fused_kernel(
    own_ref, far_ref, near_ref, lo_ref, hi_ref, flo_ref, fhi_ref, hal_ref, wf_ref, wb_ref,
    out_ref, ing_ref, wg_ref, vs_ref, cs_ref,
):
    both = own_ref.shape[0]
    loc = both // 2
    planes = out_ref.shape[1]
    width = out_ref.shape[2] * out_ref.shape[3]
    plane = width + 2 * ROW
    span = (planes - 1) * plane + width
    blank = jnp.zeros((loc, ROW), jnp.bfloat16)
    pieces = (
        (lambda c: own_ref[c, :], lambda c: lo_ref[c, :], lambda c: hi_ref[c, :]),
        (lambda c: near_ref[0, c, :], lambda c: hal_ref[0, c, :], lambda c: hal_ref[1, c, :]),
        (lambda c: far_ref[c, :], lambda c: flo_ref[c, :], lambda c: fhi_ref[c, :]),
        (lambda c: near_ref[1, c, :], lambda c: hal_ref[2, c, :], lambda c: hal_ref[3, c, :]),
    )
    for k, (body_of, low_of, high_of) in enumerate(pieces):
        rows = slice(k * loc, (k + 1) * loc)
        for ref, low in ((vs_ref, 0), (cs_ref, loc)):
            chans = slice(low, low + loc)
            for zp in range(planes + 2):
                ref[rows, zp * plane : zp * plane + ROW] = blank
                ref[rows, zp * plane + ROW + width : (zp + 1) * plane] = blank
            ref[rows, ROW : ROW + width] = low_of(chans)
            for z in range(planes):
                at = (z + 1) * plane + ROW
                ref[rows, at : at + width] = body_of(chans)[:, z * width : (z + 1) * width]
            at = (planes + 1) * plane + ROW
            ref[rows, at : at + width] = high_of(chans)
    lane = lax.broadcasted_iota(jnp.int32, (loc, span), 1) % ROW
    first = lane == 0
    last = lane == ROW - 1
    zero = jnp.zeros((loc, span), jnp.float32)
    start = plane + ROW
    cm = cs_ref[0:loc, start : start + span].astype(jnp.float32)
    c_prev = jnp.where(last, zero, pltpu.roll(cm, span - 1, 1))
    c_next = jnp.where(first, zero, pltpu.roll(cm, 1, 1))
    cstack = jnp.concatenate([c_prev, cm, c_next], axis=0).astype(jnp.bfloat16)

    def shifted_sum(r):
        left = jnp.where(first, zero, pltpu.roll(r[0:loc], 1, 1))
        right = jnp.where(last, zero, pltpu.roll(r[2 * loc : 3 * loc], span - 1, 1))
        return left + r[loc : 2 * loc] + right

    acc_o = None
    acc_i = None
    for tap_z in range(3):
        for tap_y in range(3):
            base = tap_z * plane + tap_y * ROW
            pair = 3 * tap_z + tap_y
            sv = vs_ref[:, base : base + span]
            sc = cs_ref[:, base : base + span]
            r = jnp.dot(wf_ref[pair], sv, preferred_element_type=jnp.float32)
            acc_o = r if acc_o is None else acc_o + r
            r = jnp.dot(wb_ref[pair], sc, preferred_element_type=jnp.float32)
            acc_i = r if acc_i is None else acc_i + r
            w = lax.dot_general(
                sv, cstack, (((1,), (1,)), ((), ())), preferred_element_type=jnp.float32
            )
            for tap_x in range(3):
                wg_ref[3 * pair + tap_x] = w[:, tap_x * loc : (tap_x + 1) * loc].astype(wg_ref.dtype)
    acc_o = shifted_sum(acc_o)
    acc_i = shifted_sum(acc_i)
    rows, cols = out_ref.shape[2], out_ref.shape[3]
    for z in range(planes):
        for acc, ref in ((acc_o, out_ref), (acc_i, ing_ref)):
            part = acc[:, z * plane : z * plane + width].reshape(loc, rows, cols)
            ref[:, z] = part.astype(ref.dtype)


def fused(own, far, near, low, high, far_low, far_high, halos, wf, wb, planes, width):
    both = own.shape[0]
    loc = both // 2
    cin = 4 * loc
    flat = (planes + 2) * (width + 2 * ROW)
    return pl.pallas_call(
        fused_kernel,
        out_shape=(
            jax.ShapeDtypeStruct((loc, planes, width // ROW, ROW), jnp.bfloat16),
            jax.ShapeDtypeStruct((loc, planes, width // ROW, ROW), jnp.bfloat16),
            jax.ShapeDtypeStruct((27, cin, loc), jnp.bfloat16),
        ),
        scratch_shapes=[
            pltpu.VMEM((cin, flat), jnp.bfloat16),
            pltpu.VMEM((cin, flat), jnp.bfloat16),
        ],
    )(own, far, near, low, high, far_low, far_high, halos, wf, wb)


def by_group(array, order, size, dim):
    return jnp.concatenate(
        [lax.dynamic_slice_in_dim(array, group * size, size, dim) for group in order], axis=dim
    )


def body(volume, weight, cotangent):
    in_local, planes_local, grid_rows, grid_cols = volume.shape
    out_local = cotangent.shape[0]
    my_group = lax.axis_index(CH)
    slabs = lax.axis_size("gz")
    voxels = planes_local * slabs * grid_rows * grid_cols
    width = grid_rows * grid_cols
    both = jnp.concatenate([volume, cotangent], axis=0).reshape(in_local + out_local, -1)
    far, near = CH
    swap = [(0, 1), (1, 0)]
    up = [(i, i + 1) for i in range(slabs - 1)]
    down = [(j, i) for i, j in up]
    got_far = lax.ppermute(both, far, swap)
    low = lax.ppermute(both[:, -width:], "gz", up)
    high = lax.ppermute(both[:, :width], "gz", down)
    far_low = lax.ppermute(got_far[:, -width:], "gz", up)
    far_high = lax.ppermute(got_far[:, :width], "gz", down)
    got_near = lax.ppermute(jnp.stack([both, got_far]), near, swap)
    halos = lax.ppermute(jnp.stack([low, high, far_low, far_high]), near, swap)
    groups = 4
    order = [jnp.bitwise_xor(my_group, j) for j in range(groups)]
    cin = groups * in_local
    cout = groups * out_local
    weight_cols = lax.dynamic_slice_in_dim(weight, my_group * out_local, out_local, 2)
    weight_cols = by_group(weight_cols, order, in_local, 1)
    wf = jnp.transpose(weight_cols.reshape(3, 3, 3, cin, out_local), (0, 1, 2, 4, 3))
    wf = wf.reshape(9, 3 * out_local, cin)
    weight_rows = lax.dynamic_slice_in_dim(weight, my_group * in_local, in_local, 1)
    weight_rows = by_group(weight_rows, order, out_local, 2)
    wb = weight_rows[::-1].reshape(9, 3 * in_local, cout)
    out, ing, wg = fused(
        both, got_far, got_near, low, high, far_low, far_high, halos, wf, wb, planes_local, width
    )
    wg = by_group(wg, order, in_local, 1)
    shape = (out_local, planes_local, grid_rows, grid_cols)
    out = out.reshape(shape)
    ing = ing.reshape(shape)
    weight_grad = summed_on_arrival(wg.astype(jnp.bfloat16), "gz", 1) * jnp.float32(
        1.0 / math.sqrt(voxels)
    )
    return out, ing, weight_grad


def solution(mesh):
    split = Mesh(mesh.devices.reshape(mesh.shape["gz"], 2, 2), ("gz", "ch_0", "ch_1"))
    placed = (P(CH, "gz", None, None), P(), P(CH, "gz", None, None))
    return jax.shard_map(
        body,
        mesh=split,
        in_specs=placed,
        out_specs=(P(CH, "gz", None, None), P(CH, "gz", None, None), P(None, "gz", CH)),
        check_vma=False,
    )
```

```python
import functools
import math

import jax
import jax.numpy as jnp
from jax import lax
from jax.experimental import pallas as pl
from jax.experimental.pallas import tpu as pltpu
from jax.sharding import Mesh
from jax.sharding import PartitionSpec as P

CH = ("ch_0", "ch_1")
ROW = 128


def summed_on_arrival(shard, axis, dim):
    before, after = (shard.shape[:dim], shard.shape[dim + 1 :])
    devices = lax.axis_size(axis)
    blocks = jnp.moveaxis(shard.reshape(*before, devices, -1, *after), dim, 0)
    arrived = lax.all_to_all(blocks, axis, split_axis=0, concat_axis=0, tiled=True)
    return arrived.astype(jnp.float32).sum(axis=0)

def fused_kernel(
    own_ref, far_ref, near_ref, lo_ref, hi_ref, flo_ref, fhi_ref, hal_ref, wf_ref, wb_ref,
    out_ref, ing_ref, wg_ref, vs_ref, cs_ref, *, scale,
):
    both = own_ref.shape[0]
    loc = both // 2
    planes = out_ref.shape[1]
    width = out_ref.shape[2] * out_ref.shape[3]
    plane = width + 2 * ROW
    span = (planes - 1) * plane + width
    blank = jnp.zeros((loc, ROW), jnp.bfloat16)
    pieces = (
        (lambda c: own_ref[c, :], lambda c: lo_ref[c, :], lambda c: hi_ref[c, :]),
        (lambda c: near_ref[0, c, :], lambda c: hal_ref[0, c, :], lambda c: hal_ref[1, c, :]),
        (lambda c: far_ref[c, :], lambda c: flo_ref[c, :], lambda c: fhi_ref[c, :]),
        (lambda c: near_ref[1, c, :], lambda c: hal_ref[2, c, :], lambda c: hal_ref[3, c, :]),
    )
    for k, (body_of, low_of, high_of) in enumerate(pieces):
        rows = slice(k * loc, (k + 1) * loc)
        for ref, low in ((vs_ref, 0), (cs_ref, loc)):
            chans = slice(low, low + loc)
            for zp in range(planes + 2):
                ref[rows, zp * plane : zp * plane + ROW] = blank
                ref[rows, zp * plane + ROW + width : (zp + 1) * plane] = blank
            ref[rows, ROW : ROW + width] = low_of(chans)
            for z in range(planes):
                at = (z + 1) * plane + ROW
                ref[rows, at : at + width] = body_of(chans)[:, z * width : (z + 1) * width]
            at = (planes + 1) * plane + ROW
            ref[rows, at : at + width] = high_of(chans)
    lane = lax.broadcasted_iota(jnp.int32, (loc, span), 1) % ROW
    first = lane == 0
    last = lane == ROW - 1
    zero = jnp.zeros((loc, span), jnp.float32)
    start = plane + ROW
    cm = cs_ref[0:loc, start : start + span].astype(jnp.float32)
    c_prev = jnp.where(last, zero, pltpu.roll(cm, span - 1, 1))
    c_next = jnp.where(first, zero, pltpu.roll(cm, 1, 1))
    cstack = jnp.concatenate([c_prev, cm, c_next], axis=0).astype(jnp.bfloat16)

    def shifted_sum(r):
        left = jnp.where(first, zero, pltpu.roll(r[0:loc], 1, 1))
        right = jnp.where(last, zero, pltpu.roll(r[2 * loc : 3 * loc], span - 1, 1))
        return left + r[loc : 2 * loc] + right

    acc_o = None
    acc_i = None
    for tap_z in range(3):
        for tap_y in range(3):
            base = tap_z * plane + tap_y * ROW
            pair = 3 * tap_z + tap_y
            sv = vs_ref[:, base : base + span]
            sc = cs_ref[:, base : base + span]
            r = jnp.dot(wf_ref[pair], sv, preferred_element_type=jnp.float32)
            acc_o = r if acc_o is None else acc_o + r
            r = jnp.dot(wb_ref[pair], sc, preferred_element_type=jnp.float32)
            acc_i = r if acc_i is None else acc_i + r
            w = lax.dot_general(
                sv, cstack, (((1,), (1,)), ((), ())), preferred_element_type=jnp.float32
            )
            for tap_x in range(3):
                wg_ref[3 * pair + tap_x] = (w[:, tap_x * loc : (tap_x + 1) * loc] * scale).astype(wg_ref.dtype)
    acc_o = shifted_sum(acc_o)
    acc_i = shifted_sum(acc_i)
    rows, cols = out_ref.shape[2], out_ref.shape[3]
    for z in range(planes):
        for acc, ref in ((acc_o, out_ref), (acc_i, ing_ref)):
            part = acc[:, z * plane : z * plane + width].reshape(loc, rows, cols)
            ref[:, z] = part.astype(ref.dtype)


def fused(own, far, near, low, high, far_low, far_high, halos, wf, wb, planes, width, scale):
    both = own.shape[0]
    loc = both // 2
    cin = 4 * loc
    flat = (planes + 2) * (width + 2 * ROW)
    return pl.pallas_call(
        functools.partial(fused_kernel, scale=scale),
        out_shape=(
            jax.ShapeDtypeStruct((loc, planes, width // ROW, ROW), jnp.bfloat16),
            jax.ShapeDtypeStruct((loc, planes, width // ROW, ROW), jnp.bfloat16),
            jax.ShapeDtypeStruct((27, cin, loc), jnp.bfloat16),
        ),
        scratch_shapes=[
            pltpu.VMEM((cin, flat), jnp.bfloat16),
            pltpu.VMEM((cin, flat), jnp.bfloat16),
        ],
    )(own, far, near, low, high, far_low, far_high, halos, wf, wb)


def by_group(array, order, size, dim):
    return jnp.concatenate(
        [lax.dynamic_slice_in_dim(array, group * size, size, dim) for group in order], axis=dim
    )


def body(volume, weight, cotangent):
    in_local, planes_local, grid_rows, grid_cols = volume.shape
    out_local = cotangent.shape[0]
    my_group = lax.axis_index(CH)
    slabs = lax.axis_size("gz")
    voxels = planes_local * slabs * grid_rows * grid_cols
    width = grid_rows * grid_cols
    both = jnp.concatenate([volume, cotangent], axis=0).reshape(in_local + out_local, -1)
    far, near = CH
    swap = [(0, 1), (1, 0)]
    up = [(i, i + 1) for i in range(slabs - 1)]
    down = [(j, i) for i, j in up]
    got_far = lax.ppermute(both, far, swap)
    low = lax.ppermute(both[:, -width:], "gz", up)
    high = lax.ppermute(both[:, :width], "gz", down)
    far_low = lax.ppermute(got_far[:, -width:], "gz", up)
    far_high = lax.ppermute(got_far[:, :width], "gz", down)
    got_near = lax.ppermute(jnp.stack([both, got_far]), near, swap)
    halos = lax.ppermute(jnp.stack([low, high, far_low, far_high]), near, swap)
    groups = 4
    order = [jnp.bitwise_xor(my_group, j) for j in range(groups)]
    cin = groups * in_local
    cout = groups * out_local
    weight_cols = lax.dynamic_slice_in_dim(weight, my_group * out_local, out_local, 2)
    weight_cols = by_group(weight_cols, order, in_local, 1)
    wf = jnp.transpose(weight_cols.reshape(3, 3, 3, cin, out_local), (0, 1, 2, 4, 3))
    wf = wf.reshape(9, 3 * out_local, cin)
    weight_rows = lax.dynamic_slice_in_dim(weight, my_group * in_local, in_local, 1)
    weight_rows = by_group(weight_rows, order, out_local, 2)
    wb = weight_rows[::-1].reshape(9, 3 * in_local, cout)
    out, ing, wg = fused(
        both, got_far, got_near, low, high, far_low, far_high, halos, wf, wb, planes_local, width,
        1.0 / math.sqrt(voxels),
    )
    wg = by_group(wg, order, in_local, 1)
    shape = (out_local, planes_local, grid_rows, grid_cols)
    out = out.reshape(shape)
    ing = ing.reshape(shape)
    weight_grad = summed_on_arrival(wg.astype(jnp.bfloat16), "gz", 1)
    return out, ing, weight_grad


def solution(mesh):
    split = Mesh(mesh.devices.reshape(mesh.shape["gz"], 2, 2), ("gz", "ch_0", "ch_1"))
    placed = (P(CH, "gz", None, None), P(), P(CH, "gz", None, None))
    return jax.shard_map(
        body,
        mesh=split,
        in_specs=placed,
        out_specs=(P(CH, "gz", None, None), P(CH, "gz", None, None), P(None, "gz", CH)),
        check_vma=False,
    )
```

```python
import math

import jax
import jax.numpy as jnp
from jax import lax
from jax.experimental import pallas as pl
from jax.experimental.pallas import tpu as pltpu
from jax.sharding import Mesh
from jax.sharding import PartitionSpec as P

CH = ("ch_0", "ch_1")
ROW = 128


def summed_on_arrival(shard, axis, dim):
    before, after = (shard.shape[:dim], shard.shape[dim + 1 :])
    devices = lax.axis_size(axis)
    blocks = jnp.moveaxis(shard.reshape(*before, devices, -1, *after), dim, 0)
    arrived = lax.all_to_all(blocks, axis, split_axis=0, concat_axis=0, tiled=True)
    return arrived.astype(jnp.float32).sum(axis=0)

def fused_kernel(
    own_ref, far_ref, near_ref, lo_ref, hi_ref, flo_ref, fhi_ref, hal_ref, wf_ref, wb_ref,
    out_ref, ing_ref, wg_ref, vs_ref, cs_ref,
):
    both = own_ref.shape[0]
    loc = both // 2
    planes = out_ref.shape[1]
    width = out_ref.shape[2] * out_ref.shape[3]
    plane = width + 2 * ROW
    span = (planes - 1) * plane + width
    blank = jnp.zeros((loc, ROW), jnp.bfloat16)
    pieces = (
        (lambda c: own_ref[c, :], lambda c: lo_ref[c, :], lambda c: hi_ref[c, :]),
        (lambda c: near_ref[0, c, :], lambda c: hal_ref[0, c, :], lambda c: hal_ref[1, c, :]),
        (lambda c: far_ref[c, :], lambda c: flo_ref[c, :], lambda c: fhi_ref[c, :]),
        (lambda c: near_ref[1, c, :], lambda c: hal_ref[2, c, :], lambda c: hal_ref[3, c, :]),
    )
    for k, (body_of, low_of, high_of) in enumerate(pieces):
        rows = slice(k * loc, (k + 1) * loc)
        for ref, low in ((vs_ref, 0), (cs_ref, loc)):
            chans = slice(low, low + loc)
            for zp in range(planes + 2):
                ref[rows, zp * plane : zp * plane + ROW] = blank
                ref[rows, zp * plane + ROW + width : (zp + 1) * plane] = blank
            ref[rows, ROW : ROW + width] = low_of(chans)
            for z in range(planes):
                at = (z + 1) * plane + ROW
                ref[rows, at : at + width] = body_of(chans)[:, z * width : (z + 1) * width]
            at = (planes + 1) * plane + ROW
            ref[rows, at : at + width] = high_of(chans)
    lane = lax.broadcasted_iota(jnp.int32, (loc, span), 1) % ROW
    first = lane == 0
    last = lane == ROW - 1
    zero = jnp.zeros((loc, span), jnp.float32)
    start = plane + ROW
    cm = cs_ref[0:loc, start : start + span].astype(jnp.float32)
    c_prev = jnp.where(last, zero, pltpu.roll(cm, span - 1, 1))
    c_next = jnp.where(first, zero, pltpu.roll(cm, 1, 1))
    cstack = jnp.concatenate([c_prev, cm, c_next], axis=0).astype(jnp.bfloat16)

    def shifted_sum(r):
        left = jnp.where(first, zero, pltpu.roll(r[0:loc], 1, 1))
        right = jnp.where(last, zero, pltpu.roll(r[2 * loc : 3 * loc], span - 1, 1))
        return left + r[loc : 2 * loc] + right

    acc_o = None
    acc_i = None
    for tap_z in range(3):
        for tap_y in range(3):
            base = tap_z * plane + tap_y * ROW
            pair = 3 * tap_z + tap_y
            sv = vs_ref[:, base : base + span]
            sc = cs_ref[:, base : base + span]
            r = jnp.dot(wf_ref[pair], sv, preferred_element_type=jnp.float32)
            acc_o = r if acc_o is None else acc_o + r
            r = jnp.dot(wb_ref[pair], sc, preferred_element_type=jnp.float32)
            acc_i = r if acc_i is None else acc_i + r
            w = lax.dot_general(
                sv, cstack, (((1,), (1,)), ((), ())), preferred_element_type=jnp.float32
            )
            for tap_x in range(3):
                wg_ref[3 * pair + tap_x] = w[:, tap_x * loc : (tap_x + 1) * loc].astype(wg_ref.dtype)
    acc_o = shifted_sum(acc_o)
    acc_i = shifted_sum(acc_i)
    rows, cols = out_ref.shape[2], out_ref.shape[3]
    for z in range(planes):
        for acc, ref in ((acc_o, out_ref), (acc_i, ing_ref)):
            part = acc[:, z * plane : z * plane + width].reshape(loc, rows, cols)
            ref[:, z] = part.astype(ref.dtype)


def fused(own, far, near, low, high, far_low, far_high, halos, wf, wb, planes, width):
    both = own.shape[0]
    loc = both // 2
    cin = 4 * loc
    flat = (planes + 2) * (width + 2 * ROW)
    return pl.pallas_call(
        fused_kernel,
        out_shape=(
            jax.ShapeDtypeStruct((loc, planes, width // ROW, ROW), jnp.bfloat16),
            jax.ShapeDtypeStruct((loc, planes, width // ROW, ROW), jnp.bfloat16),
            jax.ShapeDtypeStruct((27, cin, loc), jnp.bfloat16),
        ),
        scratch_shapes=[
            pltpu.VMEM((cin, flat), jnp.bfloat16),
            pltpu.VMEM((cin, flat), jnp.bfloat16),
        ],
    )(own, far, near, low, high, far_low, far_high, halos, wf, wb)


def by_group(array, order, size, dim):
    return jnp.concatenate(
        [lax.dynamic_slice_in_dim(array, group * size, size, dim) for group in order], axis=dim
    )


def body(volume, weight, cotangent):
    in_local, planes_local, grid_rows, grid_cols = volume.shape
    out_local = cotangent.shape[0]
    my_group = lax.axis_index(CH)
    slabs = lax.axis_size("gz")
    voxels = planes_local * slabs * grid_rows * grid_cols
    width = grid_rows * grid_cols
    both = jnp.concatenate([volume, cotangent], axis=0).reshape(in_local + out_local, -1)
    far, near = CH
    swap = [(0, 1), (1, 0)]
    up = [(i, i + 1) for i in range(slabs - 1)]
    down = [(j, i) for i, j in up]
    got_far = lax.ppermute(both, far, swap)
    low = lax.ppermute(both[:, -width:], "gz", up)
    high = lax.ppermute(both[:, :width], "gz", down)
    groups = 4
    order = [jnp.bitwise_xor(my_group, j) for j in range(groups)]
    cin = groups * in_local
    cout = groups * out_local
    weight_cols = lax.dynamic_slice_in_dim(weight, my_group * out_local, out_local, 2)
    weight_cols = by_group(weight_cols, order, in_local, 1)
    wf = jnp.transpose(weight_cols.reshape(3, 3, 3, cin, out_local), (0, 1, 2, 4, 3))
    wf = wf.reshape(9, 3 * out_local, cin)
    weight_rows = lax.dynamic_slice_in_dim(weight, my_group * in_local, in_local, 1)
    weight_rows = by_group(weight_rows, order, out_local, 2)
    wb = weight_rows[::-1].reshape(9, 3 * in_local, cout)
    got_far, wf, wb = lax.optimization_barrier((got_far, wf, wb))
    far_low = lax.ppermute(got_far[:, -width:], "gz", up)
    far_high = lax.ppermute(got_far[:, :width], "gz", down)
    got_near = lax.ppermute(jnp.stack([both, got_far]), near, swap)
    halos = lax.ppermute(jnp.stack([low, high, far_low, far_high]), near, swap)
    out, ing, wg = fused(
        both, got_far, got_near, low, high, far_low, far_high, halos, wf, wb, planes_local, width
    )
    wg = by_group(wg, order, in_local, 1)
    shape = (out_local, planes_local, grid_rows, grid_cols)
    out = out.reshape(shape)
    ing = ing.reshape(shape)
    weight_grad = summed_on_arrival(wg.astype(jnp.bfloat16), "gz", 1) * jnp.float32(
        1.0 / math.sqrt(voxels)
    )
    return out, ing, weight_grad


def solution(mesh):
    split = Mesh(mesh.devices.reshape(mesh.shape["gz"], 2, 2), ("gz", "ch_0", "ch_1"))
    placed = (P(CH, "gz", None, None), P(), P(CH, "gz", None, None))
    return jax.shard_map(
        body,
        mesh=split,
        in_specs=placed,
        out_specs=(P(CH, "gz", None, None), P(CH, "gz", None, None), P(None, "gz", CH)),
        check_vma=False,
    )
```
